256 devices in a mesh: lev: 16 (over y, x_hi, core), lat: 16 (over z, x_lo).
Axes of the slice: x: 4 (x_hi: 2, x_lo: 2; x = x_hi * 2 + x_lo), y: 4, z: 8, core: 2. Of those that a mesh axis runs over, the one named last changes fastest.
Arguments:
- adjoint_in: float32 [8, 128, 64, 2048], P(None, 'lev', 'lat'), may hold values from -6 to 6
- courant_lon: float32 [128, 64, 2048], P('lev', 'lat'), may hold values from -0.24 to 0.24
- courant_lat: float32 [128, 64, 2048], P('lev', 'lat'), may hold values from -0.24 to 0.24, as said below
- mass_flux: float32 [64, 2048], P('lat'), may hold values from 0.1 to 0.9
- conv_band: int32 [2, 64, 2048], P(None, 'lat'), may hold values from 48 to 128, as said below
- diff_inverse: float32 [64, 8, 16, 16], P('lat'), may hold values from 0 to 1
- obs_values: float32 [16, 16, 16, 16, 128], P('lev', 'lat'), may hold values from -6 to 6
- obs_column: int32 [16, 16, 16, 16], P('lev', 'lat'), may hold values from 0 to 511
- obs_count: int32 [16, 16, 16], P('lev', 'lat'), may hold values from 0 to 16, as said below
Outputs:
- adjoint_out: float32 [8, 128, 64, 2048], P(None, 'lev', 'lat')
The draws below stay inside these ranges and needn't reach their ends.
Inputs may be any that keep to these rules, and one draw needn't show every extreme that they name: `courant_lat`: the south face of the first latitude row carries no flow. `conv_band`: bands hold 4 to 64 levels. `obs_count`: slots at and after the count hold padding. `obs_column`: several soundings may share a column.
All inputs are finite; a program needn't handle non-finite values.
Results may differ from the reference program's by a relative error of at most 0.00007.
Values sent between devices are 32-bit elements; how exact they have to be, the bound alone decides.
No kernel may reach another device: no remote copies, remote signals or barrier semaphores. Data moves between devices by JAX's collectives and lax.ppermute only.
A program may use at most 128 MiB of HBM per device.

```python
import math
import jax
import jax.numpy as jnp
from jax import lax

TRACERS = 8
LEVELS = 128
BLK = 16
NB = 8
LAT_DEV = 4
LAT = 64
LON = 2048
COLS_BLOCK = 512
CAP = 16
ADV_STEPS = 2
N_LEV = 16
N_LAT = 16


def draw_courant_lat(key, part):
    shape = (LEVELS, LAT, LON)
    values = jax.random.uniform(key, shape, jnp.float32, -0.24, 0.24)
    rows = lax.broadcasted_iota(jnp.int32, shape, 1)
    return jnp.where(rows > 0, values, jnp.float32(0.0))


def draw_conv_band(key, part):
    first_key, second_key = jax.random.split(jax.random.fold_in(key, 11))
    upper = jax.random.randint(first_key, (LAT, LON), LEVELS - LEVELS // 8, LEVELS + 1)
    length = jax.random.randint(second_key, (LAT, LON), 4, LEVELS // 2 + 1)
    return jnp.stack([upper - length, upper]).astype(jnp.int32)


def draw_diff_inverse(key, part):
    shape = (LAT, NB, BLK, BLK)
    first_key, second_key = jax.random.split(jax.random.fold_in(key, 23))
    diagonal = jax.random.uniform(first_key, shape, jnp.float32, 0.5, 1.0)
    off_top = 0.6 / (BLK - 1)
    off_diagonal = jax.random.uniform(second_key, shape, jnp.float32, 0.0, off_top)
    is_diagonal = lax.broadcasted_iota(jnp.int32, shape, 2) == lax.broadcasted_iota(jnp.int32, shape, 3)
    return jnp.where(is_diagonal, diagonal, off_diagonal)


def draw_obs_count(key, part):
    shape = (N_LEV, N_LAT, N_LAT)
    first_key, second_key = jax.random.split(jax.random.fold_in(key, 37))
    counts = jax.random.randint(first_key, shape, 0, CAP + 1)
    busiest = jax.random.randint(second_key, (N_LEV, 1, 1), 0, N_LAT)
    destination = lax.broadcasted_iota(jnp.int32, shape, 2)
    return jnp.where(destination == busiest, CAP, counts).astype(jnp.int32)


def set_ends(entries, own_key, smallest, top_value):
    dims = entries.shape
    index_at = [jax.random.randint(jax.random.fold_in(own_key, axis), (), 0, dims[axis]) for axis in range(len(dims))]
    entries = entries.at[tuple(index_at)].set(smallest)
    longest = dims.index(max(dims))
    index_at[longest] = (index_at[longest] + 1) % dims[longest]
    return entries.at[tuple(index_at)].set(top_value)


def steps_of(rng, dims, pieces, low, largest):
    level, own = 1.0, jax.random.fold_in(rng, 6)
    for dim, blocks in pieces:
        heights = jnp.exp(jax.random.uniform(jax.random.fold_in(own, dim), (blocks,), jnp.float32, low / len(pieces), largest / len(pieces)))
        level = level * jnp.repeat(heights, dims[dim] // blocks).reshape([-1 if axis == dim else 1 for axis in range(len(dims))])
    return level


def centred(rng, dims, width, reach, pieces=(), kind=jnp.bfloat16):
    entries = width * jax.random.normal(rng, dims, jnp.float32)
    if pieces:
        entries = entries * steps_of(rng, dims, pieces, -0.22, 0.18)
    return jnp.clip(entries, -reach, reach).astype(kind)


def setup_inputs(seed: int = 0) -> dict:
    keys = jax.random.split(jax.random.key(seed), 10)
    adjoint_in = centred(keys[0], (TRACERS, LEVELS, LAT, LON), 1.0, 6.0, ((1, 16), (2, 16)), jnp.float32)
    courant_lon = jnp.clip(jax.random.uniform(keys[1], (LEVELS, LAT, LON), jnp.float32, -0.24, 0.24) * steps_of(keys[1], (LEVELS, LAT, LON), ((0, 16), (1, 16)), -0.4, 0.0), -0.24, 0.24)
    courant_lat = draw_courant_lat(jax.random.fold_in(keys[9], 71), 0)
    mass_flux = jnp.clip(jnp.exp(math.log(0.9) - 2.1972245 * jax.random.uniform(keys[3], (LAT, LON), jnp.float32) ** steps_of(keys[3], (LAT, LON), ((0, 16),), -0.2, 0.2)), 0.1, 0.9)
    conv_band = draw_conv_band(jax.random.fold_in(keys[9], 71), 0)
    diff_inverse = draw_diff_inverse(jax.random.fold_in(keys[9], 71), 0)
    obs_values = centred(keys[6], (N_LEV, N_LAT, N_LAT, CAP, LEVELS), 1.0, 6.0, ((0, 16), (1, 16)), jnp.float32)
    obs_column = set_ends(jax.random.randint(keys[7], (N_LEV, N_LAT, N_LAT, CAP), 0, COLS_BLOCK), jax.random.fold_in(keys[7], 1), 0, COLS_BLOCK - 1).astype(jnp.int32)
    obs_count = draw_obs_count(jax.random.fold_in(keys[9], 71), 0)
    return {"adjoint_in": adjoint_in, "courant_lon": courant_lon, "courant_lat": courant_lat, "mass_flux": mass_flux, "conv_band": conv_band, "diff_inverse": diff_inverse, "obs_values": obs_values, "obs_column": obs_column, "obs_count": obs_count}


def advect(padded_rows, lat_faces, lon_faces):
    row_total = lon_faces.shape[-2]
    center_rows = padded_rows[..., 1:row_total + 1, :]
    northern = padded_rows[..., 2:row_total + 2, :]
    southern = padded_rows[..., 0:row_total, :]
    face_south = lat_faces[..., 0:row_total, :]
    face_north = lat_faces[..., 1:row_total + 1, :]
    face_east = jnp.roll(lon_faces, -1, axis=-1)
    eastern = jnp.roll(center_rows, -1, axis=-1)
    western = jnp.roll(center_rows, 1, axis=-1)
    flow_east = jnp.maximum(face_east, 0.0)
    flow_west = jnp.minimum(lon_faces, 0.0)
    flow_north = jnp.maximum(face_north, 0.0)
    flow_south = jnp.minimum(face_south, 0.0)
    center = 1.0 - flow_east + flow_west - flow_north + flow_south
    return center_rows * center + eastern * flow_east - western * flow_west + northern * flow_north - southern * flow_south


def reference(adjoint_in, courant_lon, courant_lat, mass_flux, conv_band, diff_inverse, obs_values, obs_column, obs_count):
    state = adjoint_in
    lat_padded = jnp.concatenate([courant_lat, jnp.zeros_like(courant_lat[:, :1])], axis=1)
    for substep in range(ADV_STEPS):
        padded = jnp.pad(state, ((0, 0), (0, 0), (1, 1), (0, 0)))
        state = advect(padded, lat_padded, courant_lon)
    levels = jnp.arange(LEVELS, dtype=jnp.int32)[:, None, None]
    inside = ((levels >= conv_band[0][None]) & (levels < conv_band[1][None])).astype(jnp.float32)
    counted = (conv_band[1] - conv_band[0]).astype(jnp.float32)
    band_mean = jnp.sum(state * inside[None], axis=1) / counted
    state = state + mass_flux * inside[None] * (band_mean[:, None] - state)
    blocked = state.reshape(TRACERS, NB, BLK, LAT, LON)
    state = jnp.einsum("rbij,tbjrl->tbirl", diff_inverse, blocked, precision=lax.Precision.HIGHEST).reshape(TRACERS, LEVELS, LAT, LON)
    slot_ids = jnp.arange(CAP, dtype=jnp.int32)
    valid_slot = slot_ids[None, None, None, :] < obs_count[..., None]
    holder_lev = jnp.arange(N_LEV, dtype=jnp.int32)[:, None, None, None]
    dest_group = jnp.arange(N_LAT, dtype=jnp.int32)[None, None, :, None]
    target = (dest_group * (LAT_DEV * LON) + holder_lev * COLS_BLOCK + obs_column).astype(jnp.int32)
    weighted = jnp.where(valid_slot[..., None], obs_values, jnp.float32(0.0))
    forcing = jax.ops.segment_sum(weighted.reshape(-1, LEVELS), target.reshape(-1), num_segments=LAT * LON)
    forcing = forcing.T.reshape(LEVELS, LAT, LON)
    return state + forcing[None]
```

```python
import jax
import jax.numpy as jnp
from jax import lax
from jax.experimental import pallas as pl
from jax.experimental.pallas import tpu as pltpu
from jax.sharding import PartitionSpec as P


F32 = jnp.float32
LANES = 128


def split_rows(x):
    lead = x.shape[:-2]
    rows, lons = x.shape[-2:]
    x = x.reshape(*lead, rows, lons // LANES, LANES).swapaxes(-3, -2)
    return x.reshape(*lead, rows * lons // LANES, LANES)


def join_rows(x, rows, lons):
    lead = x.shape[:-2]
    x = x.reshape(*lead, lons // LANES, rows, LANES).swapaxes(-3, -2)
    return x.reshape(*lead, rows, lons)


def lane_slice(j):
    return pl.ds(j * LANES, LANES)


def swap_axes8(tiles):
    row = lax.broadcasted_iota(jnp.int32, (8, LANES), 0)
    tiles = list(tiles)
    for step in (4, 2, 1):
        low_half = (row & step) == 0
        for i in range(8):
            if i & step == 0:
                low, high = tiles[i], tiles[i + step]
                tiles[i] = jnp.where(low_half, low, pltpu.roll(high, step, 0))
                tiles[i + step] = jnp.where(low_half, pltpu.roll(low, 8 - step, 0), high)
    return tiles


def unpack_rows(source, target):
    for k in range(8):
        tiles = swap_axes8([source(level * 64 + k * 8) for level in range(8)])
        for half in range(2):
            for r in range(4):
                target[r, :, lane_slice(2 * k + half)] = tiles[4 * half + r]


def east_tiles(tiles):
    lane = lax.broadcasted_iota(jnp.int32, tiles[0].shape, 1)
    turned = [pltpu.roll(x, LANES - 1, 1) for x in tiles]
    count = len(tiles)
    return [jnp.where(lane == LANES - 1, turned[(j + 1) % count], turned[j]) for j in range(count)]


def west_tiles(tiles):
    lane = lax.broadcasted_iota(jnp.int32, tiles[0].shape, 1)
    turned = [pltpu.roll(x, 1, 1) for x in tiles]
    return [jnp.where(lane == 0, turned[j - 1], turned[j]) for j in range(len(tiles))]


def flow_coefficients(u_ref, v_ref, u_rows, v_rows, coef_ref):
    unpack_rows(lambda start: u_ref[pl.ds(start, 8), :], u_rows)
    unpack_rows(lambda start: v_ref[pl.ds(start, 8), :], v_rows)
    for r in range(4):
        u = [u_rows[r, :, lane_slice(j)] for j in range(16)]
        ue = east_tiles(u)
        for j in range(16):
            s = lane_slice(j)
            east = jnp.maximum(ue[j], 0.0)
            west = jnp.minimum(u[j], 0.0)
            south = jnp.minimum(v_rows[r, :, s], 0.0)
            center = 1.0 - east + west + south
            if r < 3:
                north = jnp.maximum(v_rows[r + 1, :, s], 0.0)
                center = center - north
                coef_ref[2, r, :, s] = north
            coef_ref[0, r, :, s] = east
            coef_ref[1, r, :, s] = west
            coef_ref[3, r, :, s] = south
            coef_ref[4, r, :, s] = center


def prep_kernel(
    a_hbm, u_hbm, v_hbm, part_hbm, north_hbm, south_hbm, coef_hbm,
    a_ref, u_ref, v_ref, rows_ref, v_rows, part_ref, north_ref, south_ref, coef_ref, sems,
):
    faces = [
        pltpu.make_async_copy(u_hbm, u_ref, sems.at[8, 2]),
        pltpu.make_async_copy(v_hbm, v_ref, sems.at[8, 3]),
    ]
    for copy in faces:
        copy.start()

    def incoming(t):
        return pltpu.make_async_copy(a_hbm.at[t], a_ref.at[t], sems.at[t, 3])

    @pl.loop(0, 8)
    def _(t):
        incoming(t).start()

    def copies(t):
        pair = pl.ds(2 * t, 2)
        return [
            pltpu.make_async_copy(part_ref.at[t], part_hbm.at[t], sems.at[t, 0]),
            pltpu.make_async_copy(north_ref.at[pair], north_hbm.at[pair], sems.at[t, 1]),
            pltpu.make_async_copy(south_ref.at[pair], south_hbm.at[pair], sems.at[t, 2]),
        ]

    for copy in faces:
        copy.wait()
    flow_coefficients(u_ref, v_ref, rows_ref, v_rows, coef_ref)
    south_ref[16] = v_rows[0]
    coef_copy = pltpu.make_async_copy(coef_ref, coef_hbm, sems.at[8, 0])
    face_copy = pltpu.make_async_copy(south_ref.at[pl.ds(16, 1)], south_hbm.at[pl.ds(16, 1)], sems.at[8, 1])
    coef_copy.start()
    face_copy.start()

    @pl.loop(0, 8)
    def _(t):
        incoming(t).wait()
        unpack_rows(lambda start: a_ref[t, pl.ds(start, 8), :], rows_ref)
        for r in range(4):
            row = [rows_ref[r, :, lane_slice(j)] for j in range(16)]
            e = east_tiles(row)
            w = west_tiles(row)
            for j in range(16):
                s = lane_slice(j)
                out = row[j] * coef_ref[4, r, :, s] + e[j] * coef_ref[0, r, :, s] - w[j] * coef_ref[1, r, :, s]
                if r < 3:
                    out = out + rows_ref[r + 1, :, s] * coef_ref[2, r, :, s]
                if r > 0:
                    out = out - rows_ref[r - 1, :, s] * coef_ref[3, r, :, s]
                part_ref[t, r, :, s] = out
                if r == 3:
                    north_ref[2 * t, :, s] = row[j]
                    north_ref[2 * t + 1, :, s] = out
                if r == 0:
                    south_ref[2 * t, :, s] = row[j]
                    south_ref[2 * t + 1, :, s] = out
        for copy in copies(t):
            copy.start()

    @pl.loop(0, 8)
    def _(t):
        for copy in copies(t):
            copy.wait()

    coef_copy.wait()
    face_copy.wait()


def advect_kernel(
    lev_ref, part_hbm, own_north_hbm, own_south_hbm, from_south_hbm, from_north_hbm, coef_hbm, band_ref,
    adv_hbm, keep_ref, send_ref,
    adv_ref, edge_ref, sum_ref, inside_ref, part_ref, own_north_ref, own_south_ref, from_south_ref, from_north_ref, coef_ref, sems,
):
    tiles = range(16)

    def copies(t):
        pair = pl.ds(2 * t, 2)
        first = pl.ds(2 * t, 1)
        return [
            pltpu.make_async_copy(part_hbm.at[t], part_ref.at[t], sems.at[t, 0]),
            pltpu.make_async_copy(own_north_hbm.at[first], own_north_ref.at[pl.ds(t, 1)], sems.at[t, 1]),
            pltpu.make_async_copy(own_south_hbm.at[first], own_south_ref.at[pl.ds(t, 1)], sems.at[t, 2]),
            pltpu.make_async_copy(from_south_hbm.at[pair], from_south_ref.at[pair], sems.at[t, 3]),
            pltpu.make_async_copy(from_north_hbm.at[pair], from_north_ref.at[pair], sems.at[t, 4]),
        ]

    fixed = [
        pltpu.make_async_copy(coef_hbm, coef_ref, sems.at[8, 0]),
        pltpu.make_async_copy(own_south_hbm.at[pl.ds(16, 1)], own_south_ref.at[pl.ds(8, 1)], sems.at[8, 1]),
        pltpu.make_async_copy(from_north_hbm.at[pl.ds(16, 1)], from_north_ref.at[pl.ds(16, 1)], sems.at[8, 2]),
    ]
    for copy in fixed:
        copy.start()

    @pl.loop(0, 8)
    def _(t):
        for copy in copies(t):
            copy.start()

    def outgoing(t):
        return pltpu.make_async_copy(adv_ref.at[:, t], adv_hbm.at[:, t], sems.at[t, 5])

    level = lax.broadcasted_iota(jnp.int32, (8, 2048), 0) + lev_ref[0] * 8
    for r in range(4):
        first = band_ref[0, r : r + 1, :]
        last = band_ref[1, r : r + 1, :]
        inside_ref[r] = jnp.where((level >= first) & (level < last), 1.0, 0.0).astype(F32)

    for copy in fixed:
        copy.wait()
    north_face = jnp.maximum(from_north_ref[16], 0.0)
    edge_ref[0] = jnp.maximum(own_south_ref[8], 0.0)
    edge_ref[1] = jnp.minimum(from_north_ref[16], 0.0)
    edge_ref[2] = north_face
    edge_ref[3] = coef_ref[4, 3] - north_face

    @pl.loop(0, 8)
    def _(t):
        for copy in copies(t):
            copy.wait()
        this_tracer = lax.broadcasted_iota(jnp.int32, (8, LANES), 0) == t
        rows = [[] for _ in range(6)]
        for j in tiles:
            s = lane_slice(j)
            a_south = from_south_ref[2 * t, :, s]
            a_last = own_north_ref[t, :, s]
            a_first = own_south_ref[t, :, s]
            rows[0].append(from_south_ref[2 * t + 1, :, s] + edge_ref[0, :, s] * (a_first - a_south))
            rows[1].append(part_ref[t, 0, :, s] - coef_ref[3, 0, :, s] * a_south)
            rows[2].append(part_ref[t, 1, :, s])
            rows[3].append(part_ref[t, 2, :, s])
            rows[4].append(part_ref[t, 3, :, s] + edge_ref[2, :, s] * (from_north_ref[2 * t, :, s] - a_last))
            rows[5].append(from_north_ref[2 * t + 1, :, s] - edge_ref[1, :, s] * a_last)
        for r in range(4):
            x = rows[r + 1]
            e = east_tiles(x)
            w = west_tiles(x)
            for j in tiles:
                s = lane_slice(j)
                center = coef_ref[4, r, :, s] if r < 3 else edge_ref[3, :, s]
                north = coef_ref[2, r, :, s] if r < 3 else edge_ref[2, :, s]
                out = (
                    x[j] * center
                    + e[j] * coef_ref[0, r, :, s]
                    - w[j] * coef_ref[1, r, :, s]
                    + rows[r + 2][j] * north
                    - rows[r][j] * coef_ref[3, r, :, s]
                )
                adv_ref[r, t, :, s] = out
                band = jnp.sum(out * inside_ref[r, :, s], axis=0, keepdims=True)
                sum_ref[r, :, s] = jnp.where(this_tracer, band, sum_ref[r, :, s])
        outgoing(t).start()

    @pl.loop(0, 8)
    def _(t):
        outgoing(t).wait()

    core = lax.rem(lev_ref[0], 2)
    keep_ref[...] = sum_ref[pl.ds(2 * core, 2)]
    send_ref[...] = sum_ref[pl.ds(2 - 2 * core, 2)]


def halves_of(x):
    high = x.astype(jnp.bfloat16)
    return high, (x - high.astype(F32)).astype(jnp.bfloat16)


def column_kernel(lev_ref, band_ref, flux_ref, inv_ref, gain_ref, matrix_ref):
    lev = lev_ref[0]
    core = lax.rem(lev, 2)
    block = lax.div(lev, 2)
    wide = (64, 128)
    row_pick = (lax.broadcasted_iota(jnp.int32, (64, 8), 0) & 7) == lax.broadcasted_iota(jnp.int32, (64, 8), 1)
    lane = lax.broadcasted_iota(jnp.int32, (16, 128), 1)
    half = jnp.where(lane < 64, core, 1 - core)
    lane_pick = half * 8 + (lane & 7) == lax.broadcasted_iota(jnp.int32, (16, 128), 0)
    same_tracer = (lax.broadcasted_iota(jnp.int32, wide, 0) >> 3) == ((lax.broadcasted_iota(jnp.int32, wide, 1) & 63) >> 3)
    row_pick = jnp.where(row_pick, 1.0, 0.0).astype(F32)
    lane_pick = jnp.where(lane_pick, 1.0, 0.0).astype(F32)
    exact = dict(precision=lax.Precision.HIGHEST, preferred_element_type=F32)
    for r in range(4):
        first = band_ref[0, r : r + 1, :]
        last = band_ref[1, r : r + 1, :]
        scaled = flux_ref[r : r + 1, :] / (last - first).astype(F32)
        inv = inv_ref[r, block, pl.ds(pl.multiple_of(core * 8, 8), 8), :]
        gain = jnp.zeros((8, 2048), F32)
        for k in range(16):
            level_k = block * 16 + k
            weight = jnp.where((first <= level_k) & (level_k < last), scaled, 0.0)
            gain = gain + inv[:, k : k + 1] * weight
        gain_ref[r] = gain
        spread = lax.dot(lax.dot(row_pick, inv, **exact), lane_pick, **exact)
        high, low = halves_of(jnp.where(same_tracer, spread, 0.0))
        matrix_ref[r, 0:64, 0:128] = high
        matrix_ref[r, 0:64, 128:256] = high
        matrix_ref[r, 64:128, 0:128] = low
        matrix_ref[r, 64:128, 128:256] = jnp.zeros_like(low)


def diffuse_kernel(lev_ref, adv_hbm, other_hbm, band_ref, flux_ref, matrix_ref, out_ref, adv_ref, other_ref, sems):
    def copies(r):
        return [
            pltpu.make_async_copy(adv_hbm.at[r], adv_ref.at[r], sems.at[r, 0]),
            pltpu.make_async_copy(other_hbm.at[r], other_ref.at[r], sems.at[r, 1]),
        ]

    for r in range(4):
        for copy in copies(r):
            copy.start()
    lev = lev_ref[0]
    level = lax.broadcasted_iota(jnp.int32, (8, 2048), 0)
    own_level = level + lev * 8
    other_level = level + (lev + 1 - 2 * lax.rem(lev, 2)) * 8
    for r in range(4):
        first = band_ref[0, r : r + 1, :]
        last = band_ref[1, r : r + 1, :]
        flux = flux_ref[r : r + 1, :]

        def rest(values, levels):
            kept = 1.0 - jnp.where((levels >= first) & (levels < last), flux, 0.0)
            return halves_of((values * kept[None]).reshape(64, 2048))

        for copy in copies(r):
            copy.wait()
        own_high, own_low = rest(adv_ref[r], own_level)
        other_high, other_low = rest(other_ref[r], other_level)
        stacked = jnp.concatenate([own_high, other_high, own_low, other_low], axis=0)
        both = lax.dot(matrix_ref[r], stacked, preferred_element_type=F32)
        out_ref[r] = both[:64] + both[64:]


def finish_kernel(lev_ref, base_ref, gain_ref, own_ref, other_ref, forcing_ref, out_ref, sum_ref, done_ref, sems):
    core = lax.rem(lev_ref[0], 2)
    for q in range(2):
        for j in range(16):
            sum_ref[2 * core + q, j] = own_ref[q, :, lane_slice(j)]
            sum_ref[2 - 2 * core + q, j] = other_ref[q, :, lane_slice(j)]

    @pl.loop(0, 8)
    def _(t):
        for k in range(8):
            tiles = []
            for j in (2 * k, 2 * k + 1):
                s = lane_slice(j)
                for r in range(4):
                    total = sum_ref[r, j, pl.ds(t, 8, stride=0), :]
                    forcing = forcing_ref[4 * r + j // 4, :, lane_slice(j % 4)]
                    tiles.append(base_ref[r, t, :, s] + gain_ref[r, :, s] * total + forcing)
            tiles = swap_axes8(tiles)
            for level in range(8):
                done_ref[t, pl.ds(level * 64 + k * 8, 8), :] = tiles[level]
        pltpu.make_async_copy(done_ref.at[t], out_ref.at[t], sems.at[t]).start()

    @pl.loop(0, 8)
    def _(t):
        pltpu.make_async_copy(done_ref.at[t], out_ref.at[t], sems.at[t]).wait()


def pack_kernel(lat_ref, count_ref, values_ref, column_ref, out_ref, line_ref):
    lat = lat_ref[0]
    slot = lax.broadcasted_iota(jnp.int32, (16, LANES), 0)
    line_ref[...] = jnp.zeros((16, LANES), F32)
    line_ref[:, 0:16] = column_ref[...].astype(F32)
    placed = pltpu.roll(line_ref[...], lax.rem(lat, 8) * 16, 1)
    low = jnp.where(lat < 8, placed, 0.0)
    high = jnp.where(lat < 8, 0.0, placed)
    for d in range(16):
        out_ref[d, 0:16, :] = jnp.where(slot < count_ref[d], values_ref[d], 0.0)
        out_ref[d, 16:24, :] = jnp.zeros((8, LANES), F32)
        out_ref[d, 16:17, :] = low[d : d + 1]
        out_ref[d, 17:18, :] = high[d : d + 1]


def forcing_kernel(packed_ref, out_ref):
    lines = packed_ref[0, 16:18, :]
    for source in range(1, 16):
        lines = lines + packed_ref[source, 16:18, :]
    total = jnp.zeros((512, LANES), F32)
    column = lax.broadcasted_iota(jnp.int32, (512, LANES), 0).astype(F32)
    for part in range(2):
        hit = jnp.where(column == lines[part : part + 1], 1.0, 0.0).astype(F32)
        values = jnp.concatenate([packed_ref[8 * part + n, 0:16, :] for n in range(8)], axis=0)
        total = total + lax.dot(hit, values, precision=lax.Precision.HIGHEST, preferred_element_type=F32)
    out_ref[...] = total.T.reshape(16, 8, 512)


def body(adjoint_in, courant_lon, courant_lat, mass_flux, conv_band, diff_inverse, obs_values, obs_column, obs_count):
    tracers, levels, rows, lons = adjoint_in.shape
    lev = lax.axis_index("lev").astype(jnp.int32).reshape(1)
    lat = lax.axis_index("lat").astype(jnp.int32).reshape(1)
    lev_count = lax.axis_size("lev")
    lat_count = lax.axis_size("lat")
    smem = pl.BlockSpec(memory_space=pltpu.SMEM)
    shape = lambda *dims: jax.ShapeDtypeStruct(dims, F32)

    a_view = split_rows(adjoint_in).reshape(tracers, 512, LANES)
    u_view = split_rows(courant_lon).reshape(512, LANES)
    v_view = split_rows(courant_lat).reshape(512, LANES)

    vmem = pl.BlockSpec(memory_space=pltpu.VMEM)
    hbm = pl.BlockSpec(memory_space=pltpu.HBM)
    small = pltpu.CompilerParams(vmem_limit_bytes=16 << 20)
    row_scratch = pltpu.VMEM((4, 8, lons), F32)

    def far(*dims):
        return pltpu.HBM(dims, F32)

    def keep_far(x):
        return pltpu.with_memory_space_constraint(x, pltpu.HBM)

    part, to_north, to_south, coef = pl.pallas_call(
        prep_kernel,
        in_specs=[hbm] * 3,
        out_specs=[hbm] * 4,
        out_shape=[far(8, 4, 8, lons), far(16, 8, lons), far(17, 8, lons), far(5, 4, 8, lons)],
        scratch_shapes=[
            pltpu.VMEM((8, 512, LANES), F32), pltpu.VMEM((512, LANES), F32), pltpu.VMEM((512, LANES), F32),
            row_scratch, row_scratch, pltpu.VMEM((8, 4, 8, lons), F32), pltpu.VMEM((16, 8, lons), F32),
            pltpu.VMEM((17, 8, lons), F32), pltpu.VMEM((5, 4, 8, lons), F32), pltpu.SemaphoreType.DMA((9, 4)),
        ],
        compiler_params=small,
    )(keep_far(a_view), keep_far(u_view), keep_far(v_view))
    from_south = lax.ppermute(to_north, "lat", [(i, i + 1) for i in range(lat_count - 1)])
    from_north = lax.ppermute(to_south, "lat", [(i + 1, i) for i in range(lat_count - 1)])

    packed = pl.pallas_call(
        pack_kernel,
        in_specs=[smem, smem, vmem, vmem],
        out_specs=vmem,
        out_shape=shape(16, 24, LANES),
        scratch_shapes=[pltpu.VMEM((16, LANES), F32)],
        compiler_params=small,
    )(lat, obs_count.reshape(16), obs_values.reshape(16, 16, LANES), obs_column.reshape(16, 16))
    packed = lax.all_to_all(packed, "lat", split_axis=0, concat_axis=0, tiled=True)

    forcing = pl.pallas_call(
        forcing_kernel, in_specs=[vmem], out_specs=vmem, out_shape=shape(16, 8, 512), compiler_params=small
    )(packed)
    forcing = lax.all_to_all(forcing, "lev", split_axis=0, concat_axis=0, tiled=True)

    gain, matrix = pl.pallas_call(
        column_kernel,
        in_specs=[smem] + [vmem] * 3,
        out_specs=[vmem] * 2,
        out_shape=[shape(4, 8, lons), jax.ShapeDtypeStruct((4, 128, 256), jnp.bfloat16)],
        compiler_params=small,
    )(lev, conv_band, mass_flux, diff_inverse)

    adv, keep, send = pl.pallas_call(
        advect_kernel,
        in_specs=[smem] + [hbm] * 6 + [vmem],
        out_specs=[hbm, vmem, vmem],
        out_shape=[far(4, 8, 8, lons), shape(2, 8, lons), shape(2, 8, lons)],
        scratch_shapes=[
            pltpu.VMEM((4, 8, 8, lons), F32), row_scratch, row_scratch, row_scratch, pltpu.VMEM((8, 4, 8, lons), F32), pltpu.VMEM((8, 8, lons), F32),
            pltpu.VMEM((9, 8, lons), F32), pltpu.VMEM((16, 8, lons), F32), pltpu.VMEM((17, 8, lons), F32),
            pltpu.VMEM((5, 4, 8, lons), F32), pltpu.SemaphoreType.DMA((9, 6)),
        ],
        compiler_params=small,
    )(lev, keep_far(part), keep_far(to_north), keep_far(to_south), from_south, from_north, keep_far(coef), conv_band)

    swap = [(i, i ^ 1) for i in range(lev_count)]
    swapped = lax.ppermute(send, "lev", swap)
    chip_sum = keep + swapped
    blocks = lev_count // 2
    pairs = [(2 * n + c, 2 * (n ^ 1) + c) for n in range(2, blocks) for c in range(2)]
    total = chip_sum + lax.ppermute(chip_sum, "lev", pairs)
    adv_out, _ = lax.optimization_barrier((adv, swapped))
    adv_other = lax.ppermute(adv_out, "lev", swap)
    lines = blocks // 2 - 1
    moved = []
    for shift in range(1, lines):
        pairs = []
        for y in range(lines):
            for n in range(4):
                pairs.append((4 * (y + 1) + n, 4 * ((y + shift) % lines + 1) + n))
        moved.append(lax.ppermute(total, "lev", pairs))
    total = sum(moved, total)
    total_other = lax.ppermute(total, "lev", swap)

    base = pl.pallas_call(
        diffuse_kernel,
        in_specs=[smem, hbm, hbm] + [vmem] * 3,
        out_specs=vmem,
        out_shape=shape(4, 64, lons),
        scratch_shapes=[pltpu.VMEM((4, 8, 8, lons), F32), pltpu.VMEM((4, 8, 8, lons), F32), pltpu.SemaphoreType.DMA((4, 2))],
        compiler_params=small,
    )(lev, keep_far(adv), keep_far(adv_other), conv_band, mass_flux, matrix)

    out = pl.pallas_call(
        finish_kernel,
        in_specs=[smem] + [vmem] * 5,
        out_specs=hbm,
        out_shape=shape(tracers, 512, LANES),
        scratch_shapes=[
            pltpu.VMEM((4, 16, 8, LANES), F32), pltpu.VMEM((8, 512, LANES), F32), pltpu.SemaphoreType.DMA((8,))
        ],
        compiler_params=small,
    )(lev, base.reshape(4, 8, 8, lons), gain, total, total_other, forcing)
    return join_rows(out.reshape(tracers, levels, 64, LANES), rows, lons)


def solution(mesh):
    placed = (
        P(None, "lev", "lat", None),
        P("lev", "lat", None),
        P("lev", "lat", None),
        P("lat", None),
        P(None, "lat", None),
        P("lat", None, None, None),
        P("lev", "lat", None, None, None),
        P("lev", "lat", None, None),
        P("lev", "lat", None),
    )

    def step(*args):
        return body(*args)

    step = jax.shard_map(
        step, mesh=mesh, in_specs=placed, out_specs=P(None, "lev", "lat", None), check_vma=False
    )
    return step
```

```python
import jax
import jax.numpy as jnp
from jax import lax
from jax.experimental import pallas as pl
from jax.experimental.pallas import tpu as pltpu
from jax.sharding import PartitionSpec as P


F32 = jnp.float32
LANES = 128


def split_rows(x):
    lead = x.shape[:-2]
    rows, lons = x.shape[-2:]
    x = x.reshape(*lead, rows, lons // LANES, LANES).swapaxes(-3, -2)
    return x.reshape(*lead, rows * lons // LANES, LANES)


def join_rows(x, rows, lons):
    lead = x.shape[:-2]
    x = x.reshape(*lead, lons // LANES, rows, LANES).swapaxes(-3, -2)
    return x.reshape(*lead, rows, lons)


def lane_slice(j):
    return pl.ds(j * LANES, LANES)


def swap_axes8(tiles):
    row = lax.broadcasted_iota(jnp.int32, (8, LANES), 0)
    tiles = list(tiles)
    for step in (4, 2, 1):
        low_half = (row & step) == 0
        for i in range(8):
            if i & step == 0:
                low, high = tiles[i], tiles[i + step]
                tiles[i] = jnp.where(low_half, low, pltpu.roll(high, step, 0))
                tiles[i + step] = jnp.where(low_half, pltpu.roll(low, 8 - step, 0), high)
    return tiles


def unpack_rows(source, target):
    for k in range(8):
        tiles = swap_axes8([source(level * 64 + k * 8) for level in range(8)])
        for half in range(2):
            for r in range(4):
                target[r, :, lane_slice(2 * k + half)] = tiles[4 * half + r]


def east_tiles(tiles):
    lane = lax.broadcasted_iota(jnp.int32, tiles[0].shape, 1)
    turned = [pltpu.roll(x, LANES - 1, 1) for x in tiles]
    count = len(tiles)
    return [jnp.where(lane == LANES - 1, turned[(j + 1) % count], turned[j]) for j in range(count)]


def west_tiles(tiles):
    lane = lax.broadcasted_iota(jnp.int32, tiles[0].shape, 1)
    turned = [pltpu.roll(x, 1, 1) for x in tiles]
    return [jnp.where(lane == 0, turned[j - 1], turned[j]) for j in range(len(tiles))]


def flow_coefficients(u_ref, v_ref, u_rows, v_rows, coef_ref):
    unpack_rows(lambda start: u_ref[pl.ds(start, 8), :], u_rows)
    unpack_rows(lambda start: v_ref[pl.ds(start, 8), :], v_rows)
    for r in range(4):
        u = [u_rows[r, :, lane_slice(j)] for j in range(16)]
        ue = east_tiles(u)
        for j in range(16):
            s = lane_slice(j)
            east = jnp.maximum(ue[j], 0.0)
            west = jnp.minimum(u[j], 0.0)
            south = jnp.minimum(v_rows[r, :, s], 0.0)
            center = 1.0 - east + west + south
            if r < 3:
                north = jnp.maximum(v_rows[r + 1, :, s], 0.0)
                center = center - north
                coef_ref[2, r, :, s] = north
            coef_ref[0, r, :, s] = east
            coef_ref[1, r, :, s] = west
            coef_ref[3, r, :, s] = south
            coef_ref[4, r, :, s] = center


def edge_kernel(a_hbm, last_hbm, first_hbm, a_ref, last_ref, first_ref, sems):
    def incoming(t):
        return pltpu.make_async_copy(a_hbm.at[t], a_ref.at[t], sems.at[t, 0])

    def outgoing(t):
        return [
            pltpu.make_async_copy(last_ref.at[t], last_hbm.at[t], sems.at[t, 1]),
            pltpu.make_async_copy(first_ref.at[t], first_hbm.at[t], sems.at[t, 2]),
        ]

    @pl.loop(0, 8)
    def _(t):
        incoming(t).start()

    @pl.loop(0, 8)
    def _(t):
        incoming(t).wait()
        for k in range(8):
            tiles = swap_axes8([a_ref[t, pl.ds(level * 64 + k * 8, 8), :] for level in range(8)])
            for half in range(2):
                first_ref[t, :, lane_slice(2 * k + half)] = tiles[4 * half]
                last_ref[t, :, lane_slice(2 * k + half)] = tiles[4 * half + 3]
        for copy in outgoing(t):
            copy.start()

    @pl.loop(0, 8)
    def _(t):
        for copy in outgoing(t):
            copy.wait()


def prep_kernel(
    a_hbm, u_hbm, v_hbm, part_hbm, north_hbm, south_hbm, coef_hbm,
    a_ref, u_ref, v_ref, rows_ref, v_rows, part_ref, coef_ref, sems,
):
    faces = [
        pltpu.make_async_copy(u_hbm, u_ref, sems.at[8, 2]),
        pltpu.make_async_copy(v_hbm, v_ref, sems.at[8, 3]),
    ]
    for copy in faces:
        copy.start()

    def incoming(t):
        return pltpu.make_async_copy(a_hbm.at[t], a_ref.at[t], sems.at[t, 3])

    @pl.loop(0, 8)
    def _(t):
        incoming(t).start()

    def copies(t):
        return [
            pltpu.make_async_copy(part_ref.at[t], part_hbm.at[t], sems.at[t, 0]),
            pltpu.make_async_copy(part_ref.at[t, 3], north_hbm.at[t], sems.at[t, 1]),
            pltpu.make_async_copy(part_ref.at[t, 0], south_hbm.at[t], sems.at[t, 2]),
        ]

    for copy in faces:
        copy.wait()
    flow_coefficients(u_ref, v_ref, rows_ref, v_rows, coef_ref)
    coef_copy = pltpu.make_async_copy(coef_ref, coef_hbm, sems.at[8, 0])
    face_copy = pltpu.make_async_copy(v_rows.at[0], south_hbm.at[8], sems.at[8, 1])
    coef_copy.start()
    face_copy.start()

    @pl.loop(0, 8)
    def _(t):
        incoming(t).wait()
        unpack_rows(lambda start: a_ref[t, pl.ds(start, 8), :], rows_ref)
        for r in range(4):
            row = [rows_ref[r, :, lane_slice(j)] for j in range(16)]
            e = east_tiles(row)
            w = west_tiles(row)
            for j in range(16):
                s = lane_slice(j)
                out = row[j] * coef_ref[4, r, :, s] + e[j] * coef_ref[0, r, :, s] - w[j] * coef_ref[1, r, :, s]
                if r < 3:
                    out = out + rows_ref[r + 1, :, s] * coef_ref[2, r, :, s]
                if r > 0:
                    out = out - rows_ref[r - 1, :, s] * coef_ref[3, r, :, s]
                part_ref[t, r, :, s] = out
        for copy in copies(t):
            copy.start()

    @pl.loop(0, 8)
    def _(t):
        for copy in copies(t):
            copy.wait()

    coef_copy.wait()
    face_copy.wait()


def advect_kernel(
    lev_ref, part_hbm, own_last_hbm, own_first_hbm, own_face_hbm, south_row_ref, south_part_ref, north_row_ref, north_part_ref,
    coef_hbm, band_ref, adv_ref, keep_ref, send_ref,
    edge_ref, sum_ref, inside_ref, part_ref, own_last_ref, own_first_ref, coef_ref, sems,
):
    tiles = range(16)

    def copies(t):
        return [
            pltpu.make_async_copy(part_hbm.at[t], part_ref.at[t], sems.at[t, 0]),
            pltpu.make_async_copy(own_last_hbm.at[t], own_last_ref.at[t], sems.at[t, 1]),
            pltpu.make_async_copy(own_first_hbm.at[t], own_first_ref.at[t], sems.at[t, 2]),
        ]

    fixed = [
        pltpu.make_async_copy(coef_hbm, coef_ref, sems.at[8, 0]),
        pltpu.make_async_copy(own_face_hbm.at[8], own_first_ref.at[8], sems.at[8, 1]),
    ]
    for copy in fixed:
        copy.start()

    @pl.loop(0, 8)
    def _(t):
        for copy in copies(t):
            copy.start()

    level = lax.broadcasted_iota(jnp.int32, (8, 2048), 0) + lev_ref[0] * 8
    for r in range(4):
        first = band_ref[0, r : r + 1, :]
        last = band_ref[1, r : r + 1, :]
        inside_ref[r] = jnp.where((level >= first) & (level < last), 1.0, 0.0).astype(F32)

    for copy in fixed:
        copy.wait()
    north_face = jnp.maximum(north_part_ref[8], 0.0)
    edge_ref[0] = jnp.maximum(own_first_ref[8], 0.0)
    edge_ref[1] = jnp.minimum(north_part_ref[8], 0.0)
    edge_ref[2] = north_face
    edge_ref[3] = coef_ref[4, 3] - north_face

    @pl.loop(0, 8)
    def _(t):
        for copy in copies(t):
            copy.wait()
        this_tracer = lax.broadcasted_iota(jnp.int32, (8, LANES), 0) == t
        rows = [[] for _ in range(6)]
        for j in tiles:
            s = lane_slice(j)
            a_south = south_row_ref[t, :, s]
            a_last = own_last_ref[t, :, s]
            a_first = own_first_ref[t, :, s]
            rows[0].append(south_part_ref[t, :, s] + edge_ref[0, :, s] * (a_first - a_south))
            rows[1].append(part_ref[t, 0, :, s] - coef_ref[3, 0, :, s] * a_south)
            rows[2].append(part_ref[t, 1, :, s])
            rows[3].append(part_ref[t, 2, :, s])
            rows[4].append(part_ref[t, 3, :, s] + edge_ref[2, :, s] * (north_row_ref[t, :, s] - a_last))
            rows[5].append(north_part_ref[t, :, s] - edge_ref[1, :, s] * a_last)
        for r in range(4):
            x = rows[r + 1]
            e = east_tiles(x)
            w = west_tiles(x)
            for j in tiles:
                s = lane_slice(j)
                center = coef_ref[4, r, :, s] if r < 3 else edge_ref[3, :, s]
                north = coef_ref[2, r, :, s] if r < 3 else edge_ref[2, :, s]
                out = (
                    x[j] * center
                    + e[j] * coef_ref[0, r, :, s]
                    - w[j] * coef_ref[1, r, :, s]
                    + rows[r + 2][j] * north
                    - rows[r][j] * coef_ref[3, r, :, s]
                )
                adv_ref[r, t, :, s] = out
                band = jnp.sum(out * inside_ref[r, :, s], axis=0, keepdims=True)
                sum_ref[r, :, s] = jnp.where(this_tracer, band, sum_ref[r, :, s])

    core = lax.rem(lev_ref[0], 2)
    keep_ref[...] = sum_ref[pl.ds(2 * core, 2)]
    send_ref[...] = sum_ref[pl.ds(2 - 2 * core, 2)]


def halves_of(x):
    high = x.astype(jnp.bfloat16)
    return high, (x - high.astype(F32)).astype(jnp.bfloat16)


def column_kernel(lev_ref, band_ref, flux_ref, inv_ref, gain_ref, matrix_ref):
    lev = lev_ref[0]
    core = lax.rem(lev, 2)
    block = lax.div(lev, 2)
    wide = (64, 128)
    row_pick = (lax.broadcasted_iota(jnp.int32, (64, 8), 0) & 7) == lax.broadcasted_iota(jnp.int32, (64, 8), 1)
    lane = lax.broadcasted_iota(jnp.int32, (16, 128), 1)
    half = jnp.where(lane < 64, core, 1 - core)
    lane_pick = half * 8 + (lane & 7) == lax.broadcasted_iota(jnp.int32, (16, 128), 0)
    same_tracer = (lax.broadcasted_iota(jnp.int32, wide, 0) >> 3) == ((lax.broadcasted_iota(jnp.int32, wide, 1) & 63) >> 3)
    row_pick = jnp.where(row_pick, 1.0, 0.0).astype(F32)
    lane_pick = jnp.where(lane_pick, 1.0, 0.0).astype(F32)
    exact = dict(precision=lax.Precision.HIGHEST, preferred_element_type=F32)
    for r in range(4):
        first = band_ref[0, r : r + 1, :]
        last = band_ref[1, r : r + 1, :]
        scaled = flux_ref[r : r + 1, :] / (last - first).astype(F32)
        inv = inv_ref[r, block, pl.ds(pl.multiple_of(core * 8, 8), 8), :]
        gain = jnp.zeros((8, 2048), F32)
        for k in range(16):
            level_k = block * 16 + k
            weight = jnp.where((first <= level_k) & (level_k < last), scaled, 0.0)
            gain = gain + inv[:, k : k + 1] * weight
        gain_ref[r] = gain
        spread = lax.dot(lax.dot(row_pick, inv, **exact), lane_pick, **exact)
        high, low = halves_of(jnp.where(same_tracer, spread, 0.0))
        matrix_ref[r, 0:64, 0:128] = high
        matrix_ref[r, 0:64, 128:256] = high
        matrix_ref[r, 64:128, 0:128] = low
        matrix_ref[r, 64:128, 128:256] = jnp.zeros_like(low)


def diffuse_kernel(lev_ref, adv_ref, other_ref, band_ref, flux_ref, matrix_ref, out_ref):
    lev = lev_ref[0]
    level = lax.broadcasted_iota(jnp.int32, (8, 2048), 0)
    own_level = level + lev * 8
    other_level = level + (lev + 1 - 2 * lax.rem(lev, 2)) * 8
    for r in range(4):
        first = band_ref[0, r : r + 1, :]
        last = band_ref[1, r : r + 1, :]
        flux = flux_ref[r : r + 1, :]

        def rest(values, levels):
            kept = 1.0 - jnp.where((levels >= first) & (levels < last), flux, 0.0)
            return halves_of((values * kept[None]).reshape(64, 2048))

        own_high, own_low = rest(adv_ref[r], own_level)
        other_high, other_low = rest(other_ref[r], other_level)
        stacked = jnp.concatenate([own_high, other_high, own_low, other_low], axis=0)
        both = lax.dot(matrix_ref[r], stacked, preferred_element_type=F32)
        out_ref[r] = both[:64] + both[64:]


def finish_kernel(lev_ref, base_ref, gain_ref, own_ref, other_ref, forcing_ref, out_ref, sum_ref, done_ref, sems):
    core = lax.rem(lev_ref[0], 2)
    for q in range(2):
        for j in range(16):
            sum_ref[2 * core + q, j] = own_ref[q, :, lane_slice(j)]
            sum_ref[2 - 2 * core + q, j] = other_ref[q, :, lane_slice(j)]

    @pl.loop(0, 8)
    def _(t):
        for k in range(8):
            tiles = []
            for j in (2 * k, 2 * k + 1):
                s = lane_slice(j)
                for r in range(4):
                    total = sum_ref[r, j, pl.ds(t, 8, stride=0), :]
                    forcing = forcing_ref[4 * r + j // 4, :, lane_slice(j % 4)]
                    tiles.append(base_ref[r, t, :, s] + gain_ref[r, :, s] * total + forcing)
            tiles = swap_axes8(tiles)
            for level in range(8):
                done_ref[t, pl.ds(level * 64 + k * 8, 8), :] = tiles[level]
        pltpu.make_async_copy(done_ref.at[t], out_ref.at[t], sems.at[t]).start()

    @pl.loop(0, 8)
    def _(t):
        pltpu.make_async_copy(done_ref.at[t], out_ref.at[t], sems.at[t]).wait()


def pack_kernel(lat_ref, count_ref, values_ref, column_ref, out_ref, line_ref):
    lat = lat_ref[0]
    slot = lax.broadcasted_iota(jnp.int32, (16, LANES), 0)
    line_ref[...] = jnp.zeros((16, LANES), F32)
    line_ref[:, 0:16] = column_ref[...].astype(F32)
    placed = pltpu.roll(line_ref[...], lax.rem(lat, 8) * 16, 1)
    low = jnp.where(lat < 8, placed, 0.0)
    high = jnp.where(lat < 8, 0.0, placed)
    for d in range(16):
        out_ref[d, 0:16, :] = jnp.where(slot < count_ref[d], values_ref[d], 0.0)
        out_ref[d, 16:24, :] = jnp.zeros((8, LANES), F32)
        out_ref[d, 16:17, :] = low[d : d + 1]
        out_ref[d, 17:18, :] = high[d : d + 1]


def forcing_kernel(packed_ref, out_ref):
    lines = packed_ref[0, 16:18, :]
    for source in range(1, 16):
        lines = lines + packed_ref[source, 16:18, :]
    total = jnp.zeros((512, LANES), F32)
    column = lax.broadcasted_iota(jnp.int32, (512, LANES), 0).astype(F32)
    for part in range(2):
        hit = jnp.where(column == lines[part : part + 1], 1.0, 0.0).astype(F32)
        values = jnp.concatenate([packed_ref[8 * part + n, 0:16, :] for n in range(8)], axis=0)
        total = total + lax.dot(hit, values, precision=lax.Precision.HIGHEST, preferred_element_type=F32)
    out_ref[...] = total.T.reshape(16, 8, 512)


def body(adjoint_in, courant_lon, courant_lat, mass_flux, conv_band, diff_inverse, obs_values, obs_column, obs_count):
    tracers, levels, rows, lons = adjoint_in.shape
    lev = lax.axis_index("lev").astype(jnp.int32).reshape(1)
    lat = lax.axis_index("lat").astype(jnp.int32).reshape(1)
    lev_count = lax.axis_size("lev")
    lat_count = lax.axis_size("lat")
    smem = pl.BlockSpec(memory_space=pltpu.SMEM)
    shape = lambda *dims: jax.ShapeDtypeStruct(dims, F32)

    a_view = split_rows(adjoint_in).reshape(tracers, 512, LANES)
    u_view = split_rows(courant_lon).reshape(512, LANES)
    v_view = split_rows(courant_lat).reshape(512, LANES)

    vmem = pl.BlockSpec(memory_space=pltpu.VMEM)
    hbm = pl.BlockSpec(memory_space=pltpu.HBM)
    small = pltpu.CompilerParams(vmem_limit_bytes=16 << 20)
    row_scratch = pltpu.VMEM((4, 8, lons), F32)

    def far(*dims):
        return pltpu.HBM(dims, F32)

    def keep_far(x):
        return pltpu.with_memory_space_constraint(x, pltpu.HBM)

    last_row, first_row = pl.pallas_call(
        edge_kernel,
        in_specs=[hbm],
        out_specs=[hbm] * 2,
        out_shape=[far(8, 8, lons), far(8, 8, lons)],
        scratch_shapes=[
            pltpu.VMEM((8, 512, LANES), F32), pltpu.VMEM((8, 8, lons), F32), pltpu.VMEM((8, 8, lons), F32),
            pltpu.SemaphoreType.DMA((8, 3)),
        ],
        compiler_params=small,
    )(keep_far(a_view))
    part, to_north, to_south, coef = pl.pallas_call(
        prep_kernel,
        in_specs=[hbm] * 3,
        out_specs=[hbm] * 4,
        out_shape=[far(8, 4, 8, lons), far(8, 8, lons), far(9, 8, lons), far(5, 4, 8, lons)],
        scratch_shapes=[
            pltpu.VMEM((8, 512, LANES), F32), pltpu.VMEM((512, LANES), F32), pltpu.VMEM((512, LANES), F32),
            row_scratch, row_scratch, pltpu.VMEM((8, 4, 8, lons), F32), pltpu.VMEM((5, 4, 8, lons), F32),
            pltpu.SemaphoreType.DMA((9, 4)),
        ],
        compiler_params=small,
    )(keep_far(a_view), keep_far(u_view), keep_far(v_view))
    north = [(i, i + 1) for i in range(lat_count - 1)]
    south = [(i + 1, i) for i in range(lat_count - 1)]
    south_row = lax.ppermute(last_row, "lat", north)
    north_row = lax.ppermute(first_row, "lat", south)
    south_part = lax.ppermute(to_north, "lat", north)
    north_part = lax.ppermute(to_south, "lat", south)

    packed = pl.pallas_call(
        pack_kernel,
        in_specs=[smem, smem, vmem, vmem],
        out_specs=vmem,
        out_shape=shape(16, 24, LANES),
        scratch_shapes=[pltpu.VMEM((16, LANES), F32)],
        compiler_params=small,
    )(lat, obs_count.reshape(16), obs_values.reshape(16, 16, LANES), obs_column.reshape(16, 16))
    packed = lax.all_to_all(packed, "lat", split_axis=0, concat_axis=0, tiled=True)

    forcing = pl.pallas_call(
        forcing_kernel, in_specs=[vmem], out_specs=vmem, out_shape=shape(16, 8, 512), compiler_params=small
    )(packed)
    forcing = lax.all_to_all(forcing, "lev", split_axis=0, concat_axis=0, tiled=True)

    gain, matrix = pl.pallas_call(
        column_kernel,
        in_specs=[smem] + [vmem] * 3,
        out_specs=[vmem] * 2,
        out_shape=[shape(4, 8, lons), jax.ShapeDtypeStruct((4, 128, 256), jnp.bfloat16)],
        compiler_params=small,
    )(lev, conv_band, mass_flux, diff_inverse)

    adv, keep, send = pl.pallas_call(
        advect_kernel,
        in_specs=[smem] + [hbm] * 4 + [vmem] * 4 + [hbm, vmem],
        out_specs=[vmem] * 3,
        out_shape=[shape(4, 8, 8, lons), shape(2, 8, lons), shape(2, 8, lons)],
        scratch_shapes=[
            row_scratch, row_scratch, row_scratch, pltpu.VMEM((8, 4, 8, lons), F32), pltpu.VMEM((8, 8, lons), F32),
            pltpu.VMEM((9, 8, lons), F32), pltpu.VMEM((5, 4, 8, lons), F32), pltpu.SemaphoreType.DMA((9, 3)),
        ],
        compiler_params=small,
    )(
        lev, keep_far(part), keep_far(last_row), keep_far(first_row), keep_far(to_south),
        south_row, south_part, north_row, north_part, keep_far(coef), conv_band,
    )

    swap = [(i, i ^ 1) for i in range(lev_count)]
    swapped = lax.ppermute(send, "lev", swap)
    chip_sum = keep + swapped
    blocks = lev_count // 2
    pairs = [(2 * n + c, 2 * (n ^ 1) + c) for n in range(2, blocks) for c in range(2)]
    total = chip_sum + lax.ppermute(chip_sum, "lev", pairs)
    adv_out, _ = lax.optimization_barrier((adv, swapped))
    adv_other = lax.ppermute(adv_out, "lev", swap)
    lines = blocks // 2 - 1
    moved = []
    for shift in range(1, lines):
        pairs = []
        for y in range(lines):
            for n in range(4):
                pairs.append((4 * (y + 1) + n, 4 * ((y + shift) % lines + 1) + n))
        moved.append(lax.ppermute(total, "lev", pairs))
    total = sum(moved, total)
    total_other = lax.ppermute(total, "lev", swap)

    base = pl.pallas_call(
        diffuse_kernel,
        in_specs=[smem] + [vmem] * 5,
        out_specs=vmem,
        out_shape=shape(4, 64, lons),
        compiler_params=small,
    )(lev, adv, adv_other, conv_band, mass_flux, matrix)

    out = pl.pallas_call(
        finish_kernel,
        in_specs=[smem] + [vmem] * 5,
        out_specs=hbm,
        out_shape=shape(tracers, 512, LANES),
        scratch_shapes=[
            pltpu.VMEM((4, 16, 8, LANES), F32), pltpu.VMEM((8, 512, LANES), F32), pltpu.SemaphoreType.DMA((8,))
        ],
        compiler_params=small,
    )(lev, base.reshape(4, 8, 8, lons), gain, total, total_other, forcing)
    return join_rows(out.reshape(tracers, levels, 64, LANES), rows, lons)


def solution(mesh):
    placed = (
        P(None, "lev", "lat", None),
        P("lev", "lat", None),
        P("lev", "lat", None),
        P("lat", None),
        P(None, "lat", None),
        P("lat", None, None, None),
        P("lev", "lat", None, None, None),
        P("lev", "lat", None, None),
        P("lev", "lat", None),
    )

    def step(*args):
        return body(*args)

    step = jax.shard_map(
        step, mesh=mesh, in_specs=placed, out_specs=P(None, "lev", "lat", None), check_vma=False
    )
    return step
```

```python
import jax
import jax.numpy as jnp
from jax import lax
from jax.experimental import pallas as pl
from jax.experimental.pallas import tpu as pltpu
from jax.sharding import PartitionSpec as P


F32 = jnp.float32
LANES = 128


def split_rows(x):
    lead = x.shape[:-2]
    rows, lons = x.shape[-2:]
    x = x.reshape(*lead, rows, lons // LANES, LANES).swapaxes(-3, -2)
    return x.reshape(*lead, rows * lons // LANES, LANES)


def join_rows(x, rows, lons):
    lead = x.shape[:-2]
    x = x.reshape(*lead, lons // LANES, rows, LANES).swapaxes(-3, -2)
    return x.reshape(*lead, rows, lons)


def lane_slice(j):
    return pl.ds(j * LANES, LANES)


def swap_axes8(tiles):
    row = lax.broadcasted_iota(jnp.int32, (8, LANES), 0)
    tiles = list(tiles)
    for step in (4, 2, 1):
        low_half = (row & step) == 0
        for i in range(8):
            if i & step == 0:
                low, high = tiles[i], tiles[i + step]
                tiles[i] = jnp.where(low_half, low, pltpu.roll(high, step, 0))
                tiles[i + step] = jnp.where(low_half, pltpu.roll(low, 8 - step, 0), high)
    return tiles


def level_sums(tiles):
    row = lax.broadcasted_iota(jnp.int32, (8, LANES), 0)
    for step in (1, 2, 4):
        low = (row & step) == 0
        tiles = [
            jnp.where(low, a, b) + pltpu.roll(jnp.where(low, b, a), step, 0) for a, b in zip(tiles[::2], tiles[1::2])
        ]
    return tiles[0]


def unpack_rows(source, target):
    for k in range(8):
        tiles = swap_axes8([source(level * 64 + k * 8) for level in range(8)])
        for half in range(2):
            for r in range(4):
                target[r, :, lane_slice(2 * k + half)] = tiles[4 * half + r]


def east_tiles(tiles):
    lane = lax.broadcasted_iota(jnp.int32, tiles[0].shape, 1)
    turned = [pltpu.roll(x, LANES - 1, 1) for x in tiles]
    count = len(tiles)
    return [jnp.where(lane == LANES - 1, turned[(j + 1) % count], turned[j]) for j in range(count)]


def west_tiles(tiles):
    lane = lax.broadcasted_iota(jnp.int32, tiles[0].shape, 1)
    turned = [pltpu.roll(x, 1, 1) for x in tiles]
    return [jnp.where(lane == 0, turned[j - 1], turned[j]) for j in range(len(tiles))]


def flow_coefficients(u_ref, v_ref, u_rows, v_rows, coef_ref):
    unpack_rows(lambda start: u_ref[pl.ds(start, 8), :], u_rows)
    unpack_rows(lambda start: v_ref[pl.ds(start, 8), :], v_rows)
    for r in range(4):
        u = [u_rows[r, :, lane_slice(j)] for j in range(16)]
        ue = east_tiles(u)
        for j in range(16):
            s = lane_slice(j)
            east = jnp.maximum(ue[j], 0.0)
            west = jnp.minimum(u[j], 0.0)
            south = jnp.minimum(v_rows[r, :, s], 0.0)
            center = 1.0 - east + west + south
            if r < 3:
                north = jnp.maximum(v_rows[r + 1, :, s], 0.0)
                center = center - north
                coef_ref[2, r, :, s] = north
            coef_ref[0, r, :, s] = east
            coef_ref[1, r, :, s] = west
            coef_ref[3, r, :, s] = south
            coef_ref[4, r, :, s] = center


def edge_kernel(a_hbm, last_hbm, first_hbm, a_ref, last_ref, first_ref, sems):
    def incoming(t):
        return pltpu.make_async_copy(a_hbm.at[t], a_ref.at[t], sems.at[t, 0])

    def outgoing(t):
        return [
            pltpu.make_async_copy(last_ref.at[t], last_hbm.at[t], sems.at[t, 1]),
            pltpu.make_async_copy(first_ref.at[t], first_hbm.at[t], sems.at[t, 2]),
        ]

    @pl.loop(0, 8)
    def _(t):
        incoming(t).start()

    @pl.loop(0, 8)
    def _(t):
        incoming(t).wait()
        for k in range(8):
            tiles = swap_axes8([a_ref[t, pl.ds(level * 64 + k * 8, 8), :] for level in range(8)])
            for half in range(2):
                first_ref[t, :, lane_slice(2 * k + half)] = tiles[4 * half]
                last_ref[t, :, lane_slice(2 * k + half)] = tiles[4 * half + 3]
        for copy in outgoing(t):
            copy.start()

    @pl.loop(0, 8)
    def _(t):
        for copy in outgoing(t):
            copy.wait()


def prep_kernel(
    a_hbm, u_hbm, v_hbm, part_hbm, north_hbm, south_hbm, coef_hbm,
    a_ref, u_ref, v_ref, rows_ref, v_rows, part_ref, coef_ref, sems,
):
    faces = [
        pltpu.make_async_copy(u_hbm, u_ref, sems.at[8, 2]),
        pltpu.make_async_copy(v_hbm, v_ref, sems.at[8, 3]),
    ]
    for copy in faces:
        copy.start()

    def incoming(t):
        return pltpu.make_async_copy(a_hbm.at[t], a_ref.at[t], sems.at[t, 3])

    @pl.loop(0, 8)
    def _(t):
        incoming(t).start()

    def copies(t):
        return [
            pltpu.make_async_copy(part_ref.at[t], part_hbm.at[t], sems.at[t, 0]),
            pltpu.make_async_copy(part_ref.at[t, 3], north_hbm.at[t], sems.at[t, 1]),
            pltpu.make_async_copy(part_ref.at[t, 0], south_hbm.at[t], sems.at[t, 2]),
        ]

    for copy in faces:
        copy.wait()
    flow_coefficients(u_ref, v_ref, rows_ref, v_rows, coef_ref)
    coef_copy = pltpu.make_async_copy(coef_ref, coef_hbm, sems.at[8, 0])
    face_copy = pltpu.make_async_copy(v_rows.at[0], south_hbm.at[8], sems.at[8, 1])
    coef_copy.start()
    face_copy.start()

    @pl.loop(0, 8)
    def _(t):
        incoming(t).wait()
        unpack_rows(lambda start: a_ref[t, pl.ds(start, 8), :], rows_ref)
        for r in range(4):
            row = [rows_ref[r, :, lane_slice(j)] for j in range(16)]
            e = east_tiles(row)
            w = west_tiles(row)
            for j in range(16):
                s = lane_slice(j)
                out = row[j] * coef_ref[4, r, :, s] + e[j] * coef_ref[0, r, :, s] - w[j] * coef_ref[1, r, :, s]
                if r < 3:
                    out = out + rows_ref[r + 1, :, s] * coef_ref[2, r, :, s]
                if r > 0:
                    out = out - rows_ref[r - 1, :, s] * coef_ref[3, r, :, s]
                part_ref[t, r, :, s] = out
        for copy in copies(t):
            copy.start()

    @pl.loop(0, 8)
    def _(t):
        for copy in copies(t):
            copy.wait()

    coef_copy.wait()
    face_copy.wait()


def advect_kernel(
    lev_ref, part_hbm, own_last_hbm, own_first_hbm, own_face_hbm, south_row_ref, south_part_ref, north_row_ref, north_part_ref,
    coef_hbm, band_ref, adv_ref, keep_ref, send_ref,
    edge_ref, sum_ref, inside_ref, part_ref, own_last_ref, own_first_ref, coef_ref, sems,
):
    tiles = range(16)

    def copies(t):
        return [
            pltpu.make_async_copy(part_hbm.at[t], part_ref.at[t], sems.at[t, 0]),
            pltpu.make_async_copy(own_last_hbm.at[t], own_last_ref.at[t], sems.at[t, 1]),
            pltpu.make_async_copy(own_first_hbm.at[t], own_first_ref.at[t], sems.at[t, 2]),
        ]

    fixed = [
        pltpu.make_async_copy(coef_hbm, coef_ref, sems.at[8, 0]),
        pltpu.make_async_copy(own_face_hbm.at[8], own_first_ref.at[8], sems.at[8, 1]),
    ]
    for copy in fixed:
        copy.start()

    @pl.loop(0, 8)
    def _(t):
        for copy in copies(t):
            copy.start()

    level = lax.broadcasted_iota(jnp.int32, (8, 2048), 0) + lev_ref[0] * 8
    for r in range(4):
        first = band_ref[0, r : r + 1, :]
        last = band_ref[1, r : r + 1, :]
        inside_ref[r] = jnp.where((level >= first) & (level < last), 1.0, 0.0).astype(F32)

    for copy in fixed:
        copy.wait()
    north_face = jnp.maximum(north_part_ref[8], 0.0)
    edge_ref[0] = jnp.maximum(own_first_ref[8], 0.0)
    edge_ref[1] = jnp.minimum(north_part_ref[8], 0.0)
    edge_ref[2] = north_face
    edge_ref[3] = coef_ref[4, 3] - north_face

    @pl.loop(0, 8)
    def _(t):
        for copy in copies(t):
            copy.wait()
        rows = [[] for _ in range(6)]
        for j in tiles:
            s = lane_slice(j)
            a_south = south_row_ref[t, :, s]
            a_last = own_last_ref[t, :, s]
            a_first = own_first_ref[t, :, s]
            rows[0].append(south_part_ref[t, :, s] + edge_ref[0, :, s] * (a_first - a_south))
            rows[1].append(part_ref[t, 0, :, s] - coef_ref[3, 0, :, s] * a_south)
            rows[2].append(part_ref[t, 1, :, s])
            rows[3].append(part_ref[t, 2, :, s])
            rows[4].append(part_ref[t, 3, :, s] + edge_ref[2, :, s] * (north_row_ref[t, :, s] - a_last))
            rows[5].append(north_part_ref[t, :, s] - edge_ref[1, :, s] * a_last)
        for r in range(4):
            x = rows[r + 1]
            e = east_tiles(x)
            w = west_tiles(x)
            for j in tiles:
                s = lane_slice(j)
                center = coef_ref[4, r, :, s] if r < 3 else edge_ref[3, :, s]
                north = coef_ref[2, r, :, s] if r < 3 else edge_ref[2, :, s]
                out = (
                    x[j] * center
                    + e[j] * coef_ref[0, r, :, s]
                    - w[j] * coef_ref[1, r, :, s]
                    + rows[r + 2][j] * north
                    - rows[r][j] * coef_ref[3, r, :, s]
                )
                adv_ref[r, t, :, s] = out

    @pl.loop(0, 4)
    def _(r):
        for j in tiles:
            s = lane_slice(j)
            inside = inside_ref[r, :, s]
            sum_ref[r, :, s] = level_sums([adv_ref[r, t, :, s] * inside for t in range(8)])

    core = lax.rem(lev_ref[0], 2)
    keep_ref[...] = sum_ref[pl.ds(2 * core, 2)]
    send_ref[...] = sum_ref[pl.ds(2 - 2 * core, 2)]


def halves_of(x):
    high = x.astype(jnp.bfloat16)
    return high, (x - high.astype(F32)).astype(jnp.bfloat16)


def column_kernel(lev_ref, band_ref, flux_ref, inv_ref, gain_ref, matrix_ref):
    lev = lev_ref[0]
    core = lax.rem(lev, 2)
    block = lax.div(lev, 2)
    wide = (64, 128)
    row_pick = (lax.broadcasted_iota(jnp.int32, (64, 8), 0) & 7) == lax.broadcasted_iota(jnp.int32, (64, 8), 1)
    lane = lax.broadcasted_iota(jnp.int32, (16, 128), 1)
    half = jnp.where(lane < 64, core, 1 - core)
    lane_pick = half * 8 + (lane & 7) == lax.broadcasted_iota(jnp.int32, (16, 128), 0)
    same_tracer = (lax.broadcasted_iota(jnp.int32, wide, 0) >> 3) == ((lax.broadcasted_iota(jnp.int32, wide, 1) & 63) >> 3)
    row_pick = jnp.where(row_pick, 1.0, 0.0).astype(F32)
    lane_pick = jnp.where(lane_pick, 1.0, 0.0).astype(F32)
    exact = dict(precision=lax.Precision.HIGHEST, preferred_element_type=F32)
    for r in range(4):
        first = band_ref[0, r : r + 1, :]
        last = band_ref[1, r : r + 1, :]
        scaled = flux_ref[r : r + 1, :] / (last - first).astype(F32)
        inv = inv_ref[r, block, pl.ds(pl.multiple_of(core * 8, 8), 8), :]
        gain = jnp.zeros((8, 2048), F32)
        for k in range(16):
            level_k = block * 16 + k
            weight = jnp.where((first <= level_k) & (level_k < last), scaled, 0.0)
            gain = gain + inv[:, k : k + 1] * weight
        gain_ref[r] = gain
        spread = lax.dot(lax.dot(row_pick, inv, **exact), lane_pick, **exact)
        high, low = halves_of(jnp.where(same_tracer, spread, 0.0))
        matrix_ref[r, 0:64, 0:128] = high
        matrix_ref[r, 0:64, 128:256] = high
        matrix_ref[r, 64:128, 0:128] = low
        matrix_ref[r, 64:128, 128:256] = jnp.zeros_like(low)


def diffuse_kernel(lev_ref, adv_ref, other_ref, band_ref, flux_ref, matrix_ref, out_ref):
    lev = lev_ref[0]
    level = lax.broadcasted_iota(jnp.int32, (8, 2048), 0)
    own_level = level + lev * 8
    other_level = level + (lev + 1 - 2 * lax.rem(lev, 2)) * 8
    for r in range(4):
        first = band_ref[0, r : r + 1, :]
        last = band_ref[1, r : r + 1, :]
        flux = flux_ref[r : r + 1, :]

        def rest(values, levels):
            kept = 1.0 - jnp.where((levels >= first) & (levels < last), flux, 0.0)
            return halves_of((values * kept[None]).reshape(64, 2048))

        own_high, own_low = rest(adv_ref[r], own_level)
        other_high, other_low = rest(other_ref[r], other_level)
        stacked = jnp.concatenate([own_high, other_high, own_low, other_low], axis=0)
        both = lax.dot(matrix_ref[r], stacked, preferred_element_type=F32)
        out_ref[r] = both[:64] + both[64:]


def finish_kernel(lev_ref, base_ref, gain_ref, own_ref, other_ref, forcing_ref, out_ref, sum_ref, done_ref, sems):
    core = lax.rem(lev_ref[0], 2)
    for q in range(2):
        for j in range(16):
            sum_ref[2 * core + q, j] = own_ref[q, :, lane_slice(j)]
            sum_ref[2 - 2 * core + q, j] = other_ref[q, :, lane_slice(j)]

    @pl.loop(0, 8)
    def _(t):
        for k in range(8):
            tiles = []
            for j in (2 * k, 2 * k + 1):
                s = lane_slice(j)
                for r in range(4):
                    total = sum_ref[r, j, pl.ds(t, 8, stride=0), :]
                    forcing = forcing_ref[4 * r + j // 4, :, lane_slice(j % 4)]
                    tiles.append(base_ref[r, t, :, s] + gain_ref[r, :, s] * total + forcing)
            tiles = swap_axes8(tiles)
            for level in range(8):
                done_ref[t, pl.ds(level * 64 + k * 8, 8), :] = tiles[level]
        pltpu.make_async_copy(done_ref.at[t], out_ref.at[t], sems.at[t]).start()

    @pl.loop(0, 8)
    def _(t):
        pltpu.make_async_copy(done_ref.at[t], out_ref.at[t], sems.at[t]).wait()


def pack_kernel(lat_ref, count_ref, values_ref, column_ref, out_ref, line_ref):
    lat = lat_ref[0]
    slot = lax.broadcasted_iota(jnp.int32, (16, LANES), 0)
    line_ref[...] = jnp.zeros((16, LANES), F32)
    line_ref[:, 0:16] = column_ref[...].astype(F32)
    placed = pltpu.roll(line_ref[...], lax.rem(lat, 8) * 16, 1)
    low = jnp.where(lat < 8, placed, 0.0)
    high = jnp.where(lat < 8, 0.0, placed)
    for d in range(16):
        out_ref[d, 0:16, :] = jnp.where(slot < count_ref[d], values_ref[d], 0.0)
        out_ref[d, 16:24, :] = jnp.zeros((8, LANES), F32)
        out_ref[d, 16:17, :] = low[d : d + 1]
        out_ref[d, 17:18, :] = high[d : d + 1]


def forcing_kernel(packed_ref, out_ref):
    lines = packed_ref[0, 16:18, :]
    for source in range(1, 16):
        lines = lines + packed_ref[source, 16:18, :]
    total = jnp.zeros((512, LANES), F32)
    column = lax.broadcasted_iota(jnp.int32, (512, LANES), 0).astype(F32)
    for part in range(2):
        hit = jnp.where(column == lines[part : part + 1], 1.0, 0.0).astype(F32)
        values = jnp.concatenate([packed_ref[8 * part + n, 0:16, :] for n in range(8)], axis=0)
        total = total + lax.dot(hit, values, precision=lax.Precision.HIGHEST, preferred_element_type=F32)
    out_ref[...] = total.T.reshape(16, 8, 512)


def body(adjoint_in, courant_lon, courant_lat, mass_flux, conv_band, diff_inverse, obs_values, obs_column, obs_count):
    tracers, levels, rows, lons = adjoint_in.shape
    lev = lax.axis_index("lev").astype(jnp.int32).reshape(1)
    lat = lax.axis_index("lat").astype(jnp.int32).reshape(1)
    lev_count = lax.axis_size("lev")
    lat_count = lax.axis_size("lat")
    smem = pl.BlockSpec(memory_space=pltpu.SMEM)
    shape = lambda *dims: jax.ShapeDtypeStruct(dims, F32)

    a_view = split_rows(adjoint_in).reshape(tracers, 512, LANES)
    u_view = split_rows(courant_lon).reshape(512, LANES)
    v_view = split_rows(courant_lat).reshape(512, LANES)

    vmem = pl.BlockSpec(memory_space=pltpu.VMEM)
    hbm = pl.BlockSpec(memory_space=pltpu.HBM)
    small = pltpu.CompilerParams(vmem_limit_bytes=16 << 20)
    row_scratch = pltpu.VMEM((4, 8, lons), F32)

    def far(*dims):
        return pltpu.HBM(dims, F32)

    def keep_far(x):
        return pltpu.with_memory_space_constraint(x, pltpu.HBM)

    last_row, first_row = pl.pallas_call(
        edge_kernel,
        in_specs=[hbm],
        out_specs=[hbm] * 2,
        out_shape=[far(8, 8, lons), far(8, 8, lons)],
        scratch_shapes=[
            pltpu.VMEM((8, 512, LANES), F32), pltpu.VMEM((8, 8, lons), F32), pltpu.VMEM((8, 8, lons), F32),
            pltpu.SemaphoreType.DMA((8, 3)),
        ],
        compiler_params=small,
    )(keep_far(a_view))
    part, to_north, to_south, coef = pl.pallas_call(
        prep_kernel,
        in_specs=[hbm] * 3,
        out_specs=[hbm] * 4,
        out_shape=[far(8, 4, 8, lons), far(8, 8, lons), far(9, 8, lons), far(5, 4, 8, lons)],
        scratch_shapes=[
            pltpu.VMEM((8, 512, LANES), F32), pltpu.VMEM((512, LANES), F32), pltpu.VMEM((512, LANES), F32),
            row_scratch, row_scratch, pltpu.VMEM((8, 4, 8, lons), F32), pltpu.VMEM((5, 4, 8, lons), F32),
            pltpu.SemaphoreType.DMA((9, 4)),
        ],
        compiler_params=small,
    )(keep_far(a_view), keep_far(u_view), keep_far(v_view))
    north = [(i, i + 1) for i in range(lat_count - 1)]
    south = [(i + 1, i) for i in range(lat_count - 1)]
    south_row = lax.ppermute(last_row, "lat", north)
    north_row = lax.ppermute(first_row, "lat", south)
    south_part = lax.ppermute(to_north, "lat", north)
    north_part = lax.ppermute(to_south, "lat", south)

    packed = pl.pallas_call(
        pack_kernel,
        in_specs=[smem, smem, vmem, vmem],
        out_specs=vmem,
        out_shape=shape(16, 24, LANES),
        scratch_shapes=[pltpu.VMEM((16, LANES), F32)],
        compiler_params=small,
    )(lat, obs_count.reshape(16), obs_values.reshape(16, 16, LANES), obs_column.reshape(16, 16))
    packed = lax.all_to_all(packed, "lat", split_axis=0, concat_axis=0, tiled=True)

    forcing = pl.pallas_call(
        forcing_kernel, in_specs=[vmem], out_specs=vmem, out_shape=shape(16, 8, 512), compiler_params=small
    )(packed)
    forcing = lax.all_to_all(forcing, "lev", split_axis=0, concat_axis=0, tiled=True)

    gain, matrix = pl.pallas_call(
        column_kernel,
        in_specs=[smem] + [vmem] * 3,
        out_specs=[vmem] * 2,
        out_shape=[shape(4, 8, lons), jax.ShapeDtypeStruct((4, 128, 256), jnp.bfloat16)],
        compiler_params=small,
    )(lev, conv_band, mass_flux, diff_inverse)

    adv, keep, send = pl.pallas_call(
        advect_kernel,
        in_specs=[smem] + [hbm] * 4 + [vmem] * 4 + [hbm, vmem],
        out_specs=[vmem] * 3,
        out_shape=[shape(4, 8, 8, lons), shape(2, 8, lons), shape(2, 8, lons)],
        scratch_shapes=[
            row_scratch, row_scratch, row_scratch, pltpu.VMEM((8, 4, 8, lons), F32), pltpu.VMEM((8, 8, lons), F32),
            pltpu.VMEM((9, 8, lons), F32), pltpu.VMEM((5, 4, 8, lons), F32), pltpu.SemaphoreType.DMA((9, 3)),
        ],
        compiler_params=small,
    )(
        lev, keep_far(part), keep_far(last_row), keep_far(first_row), keep_far(to_south),
        south_row, south_part, north_row, north_part, keep_far(coef), conv_band,
    )

    swap = [(i, i ^ 1) for i in range(lev_count)]
    swapped = lax.ppermute(send, "lev", swap)
    chip_sum = keep + swapped
    blocks = lev_count // 2
    lines = blocks // 2 - 1
    moved = []
    for shift in range(1, lines):
        pairs = []
        for y in range(lines):
            for n in range(4):
                pairs.append((4 * (y + 1) + n, 4 * ((y + shift) % lines + 1) + n))
        moved.append(lax.ppermute(chip_sum, "lev", pairs))
    total = sum(moved, chip_sum)
    adv_other = lax.ppermute(adv, "lev", swap)
    pairs = [(2 * n + c, 2 * (n ^ 1) + c) for n in range(2, blocks) for c in range(2)]
    total = total + lax.ppermute(total, "lev", pairs)
    total_other = lax.ppermute(total, "lev", swap)

    base = pl.pallas_call(
        diffuse_kernel,
        in_specs=[smem] + [vmem] * 5,
        out_specs=vmem,
        out_shape=shape(4, 64, lons),
        compiler_params=small,
    )(lev, adv, adv_other, conv_band, mass_flux, matrix)

    out = pl.pallas_call(
        finish_kernel,
        in_specs=[smem] + [vmem] * 5,
        out_specs=hbm,
        out_shape=shape(tracers, 512, LANES),
        scratch_shapes=[
            pltpu.VMEM((4, 16, 8, LANES), F32), pltpu.VMEM((8, 512, LANES), F32), pltpu.SemaphoreType.DMA((8,))
        ],
        compiler_params=small,
    )(lev, base.reshape(4, 8, 8, lons), gain, total, total_other, forcing)
    return join_rows(out.reshape(tracers, levels, 64, LANES), rows, lons)


def solution(mesh):
    placed = (
        P(None, "lev", "lat", None),
        P("lev", "lat", None),
        P("lev", "lat", None),
        P("lat", None),
        P(None, "lat", None),
        P("lat", None, None, None),
        P("lev", "lat", None, None, None),
        P("lev", "lat", None, None),
        P("lev", "lat", None),
    )

    def step(*args):
        return body(*args)

    step = jax.shard_map(
        step, mesh=mesh, in_specs=placed, out_specs=P(None, "lev", "lat", None), check_vma=False
    )
    return step
```

```python
import jax
import jax.numpy as jnp
from jax import lax
from jax.experimental import pallas as pl
from jax.experimental.pallas import tpu as pltpu
from jax.sharding import PartitionSpec as P


F32 = jnp.float32
LANES = 128


def split_rows(x):
    lead = x.shape[:-2]
    rows, lons = x.shape[-2:]
    x = x.reshape(*lead, rows, lons // LANES, LANES).swapaxes(-3, -2)
    return x.reshape(*lead, rows * lons // LANES, LANES)


def join_rows(x, rows, lons):
    lead = x.shape[:-2]
    x = x.reshape(*lead, lons // LANES, rows, LANES).swapaxes(-3, -2)
    return x.reshape(*lead, rows, lons)


def lane_slice(j):
    return pl.ds(j * LANES, LANES)


def swap_axes8(tiles):
    row = lax.broadcasted_iota(jnp.int32, (8, LANES), 0)
    tiles = list(tiles)
    for step in (4, 2, 1):
        low_half = (row & step) == 0
        for i in range(8):
            if i & step == 0:
                low, high = tiles[i], tiles[i + step]
                tiles[i] = jnp.where(low_half, low, pltpu.roll(high, step, 0))
                tiles[i + step] = jnp.where(low_half, pltpu.roll(low, 8 - step, 0), high)
    return tiles


def level_sums(tiles):
    row = lax.broadcasted_iota(jnp.int32, (8, LANES), 0)
    for step in (1, 2, 4):
        low = (row & step) == 0
        tiles = [
            jnp.where(low, a, b) + pltpu.roll(jnp.where(low, b, a), step, 0) for a, b in zip(tiles[::2], tiles[1::2])
        ]
    return tiles[0]


def unpack_rows(source, target):
    for k in range(8):
        tiles = swap_axes8([source(level * 64 + k * 8) for level in range(8)])
        for half in range(2):
            for r in range(4):
                target[r, :, lane_slice(2 * k + half)] = tiles[4 * half + r]


def east_tiles(tiles):
    lane = lax.broadcasted_iota(jnp.int32, tiles[0].shape, 1)
    turned = [pltpu.roll(x, LANES - 1, 1) for x in tiles]
    count = len(tiles)
    return [jnp.where(lane == LANES - 1, turned[(j + 1) % count], turned[j]) for j in range(count)]


def west_tiles(tiles):
    lane = lax.broadcasted_iota(jnp.int32, tiles[0].shape, 1)
    turned = [pltpu.roll(x, 1, 1) for x in tiles]
    return [jnp.where(lane == 0, turned[j - 1], turned[j]) for j in range(len(tiles))]


def flow_coefficients(u_ref, v_ref, u_rows, v_rows, coef_ref):
    unpack_rows(lambda start: u_ref[pl.ds(start, 8), :], u_rows)
    unpack_rows(lambda start: v_ref[pl.ds(start, 8), :], v_rows)
    for r in range(4):
        u = [u_rows[r, :, lane_slice(j)] for j in range(16)]
        ue = east_tiles(u)
        for j in range(16):
            s = lane_slice(j)
            east = jnp.maximum(ue[j], 0.0)
            west = jnp.minimum(u[j], 0.0)
            south = jnp.minimum(v_rows[r, :, s], 0.0)
            center = 1.0 - east + west + south
            if r < 3:
                north = jnp.maximum(v_rows[r + 1, :, s], 0.0)
                center = center - north
                coef_ref[2, r, :, s] = north
            coef_ref[0, r, :, s] = east
            coef_ref[1, r, :, s] = west
            coef_ref[3, r, :, s] = south
            coef_ref[4, r, :, s] = center


def edge_kernel(a_hbm, v_hbm, last_hbm, first_hbm, a_ref, v_ref, last_ref, first_ref, sems):
    def incoming(t):
        return pltpu.make_async_copy(a_hbm.at[t], a_ref.at[t], sems.at[t, 0])

    def outgoing(t):
        return [
            pltpu.make_async_copy(last_ref.at[t], last_hbm.at[t], sems.at[t, 1]),
            pltpu.make_async_copy(first_ref.at[t], first_hbm.at[t], sems.at[t, 2]),
        ]

    faces_in = pltpu.make_async_copy(v_hbm, v_ref, sems.at[8, 0])
    faces_out = pltpu.make_async_copy(first_ref.at[8], first_hbm.at[8], sems.at[8, 1])
    faces_in.start()

    @pl.loop(0, 8)
    def _(t):
        incoming(t).start()

    faces_in.wait()
    for k in range(8):
        tiles = swap_axes8([v_ref[pl.ds(level * 64 + k * 8, 8), :] for level in range(8)])
        for half in range(2):
            first_ref[8, :, lane_slice(2 * k + half)] = tiles[4 * half]
    faces_out.start()

    @pl.loop(0, 8)
    def _(t):
        incoming(t).wait()
        for k in range(8):
            tiles = swap_axes8([a_ref[t, pl.ds(level * 64 + k * 8, 8), :] for level in range(8)])
            for half in range(2):
                first_ref[t, :, lane_slice(2 * k + half)] = tiles[4 * half]
                last_ref[t, :, lane_slice(2 * k + half)] = tiles[4 * half + 3]
        for copy in outgoing(t):
            copy.start()

    @pl.loop(0, 8)
    def _(t):
        for copy in outgoing(t):
            copy.wait()

    faces_out.wait()


def prep_kernel(
    a_hbm, u_hbm, v_hbm, part_hbm, north_hbm, south_hbm, coef_hbm,
    a_ref, u_ref, v_ref, rows_ref, v_rows, part_ref, coef_ref, sems,
):
    faces = [
        pltpu.make_async_copy(u_hbm, u_ref, sems.at[8, 2]),
        pltpu.make_async_copy(v_hbm, v_ref, sems.at[8, 3]),
    ]
    for copy in faces:
        copy.start()

    def incoming(t):
        return pltpu.make_async_copy(a_hbm.at[t], a_ref.at[t], sems.at[t, 3])

    @pl.loop(0, 8)
    def _(t):
        incoming(t).start()

    def copies(t):
        return [
            pltpu.make_async_copy(part_ref.at[t], part_hbm.at[t], sems.at[t, 0]),
            pltpu.make_async_copy(part_ref.at[t, 3], north_hbm.at[t], sems.at[t, 1]),
            pltpu.make_async_copy(part_ref.at[t, 0], south_hbm.at[t], sems.at[t, 2]),
        ]

    for copy in faces:
        copy.wait()
    flow_coefficients(u_ref, v_ref, rows_ref, v_rows, coef_ref)
    coef_copy = pltpu.make_async_copy(coef_ref, coef_hbm, sems.at[8, 0])
    coef_copy.start()

    @pl.loop(0, 8)
    def _(t):
        incoming(t).wait()
        unpack_rows(lambda start: a_ref[t, pl.ds(start, 8), :], rows_ref)
        for r in range(4):
            row = [rows_ref[r, :, lane_slice(j)] for j in range(16)]
            e = east_tiles(row)
            w = west_tiles(row)
            for j in range(16):
                s = lane_slice(j)
                out = row[j] * coef_ref[4, r, :, s] + e[j] * coef_ref[0, r, :, s] - w[j] * coef_ref[1, r, :, s]
                if r < 3:
                    out = out + rows_ref[r + 1, :, s] * coef_ref[2, r, :, s]
                if r > 0:
                    out = out - rows_ref[r - 1, :, s] * coef_ref[3, r, :, s]
                part_ref[t, r, :, s] = out
        for copy in copies(t):
            copy.start()

    @pl.loop(0, 8)
    def _(t):
        for copy in copies(t):
            copy.wait()

    coef_copy.wait()


def inside_band(lev_ref, band_ref, r):
    level = lax.broadcasted_iota(jnp.int32, (8, 2048), 0) + lev_ref[0] * 8
    first = band_ref[0, r : r + 1, :]
    last = band_ref[1, r : r + 1, :]
    return jnp.where((level >= first) & (level < last), 1.0, 0.0).astype(F32)


def mid_kernel(
    lev_ref, part_hbm, own_last_hbm, south_row_ref, north_row_ref, coef_hbm, band_ref,
    mid_hbm, edge_hbm, flow_hbm, sum_out_ref,
    part_ref, own_last_ref, coef_ref, flow_ref, center_ref, inside_ref, mid_ref, edge_ref, sems,
):
    tiles = range(16)

    def incoming(t):
        return [
            pltpu.make_async_copy(part_hbm.at[t], part_ref.at[t], sems.at[t, 0]),
            pltpu.make_async_copy(own_last_hbm.at[t], own_last_ref.at[t], sems.at[t, 1]),
        ]

    def outgoing(t):
        return [
            pltpu.make_async_copy(mid_ref.at[:, t], mid_hbm.at[:, t], sems.at[t, 2]),
            pltpu.make_async_copy(edge_ref.at[:, t], edge_hbm.at[:, t], sems.at[t, 3]),
        ]

    coef_copy = pltpu.make_async_copy(coef_hbm, coef_ref, sems.at[8, 0])
    flow_copy = pltpu.make_async_copy(flow_ref, flow_hbm, sems.at[8, 1])
    coef_copy.start()

    @pl.loop(0, 8)
    def _(t):
        for copy in incoming(t):
            copy.start()

    for q in range(2):
        inside_ref[q] = inside_band(lev_ref, band_ref, q + 1)
    coef_copy.wait()
    north = jnp.maximum(north_row_ref[8], 0.0)
    flow_ref[0] = coef_ref[3, 0]
    flow_ref[1] = north
    center_ref[...] = coef_ref[4, 3] - north
    flow_copy.start()

    @pl.loop(0, 8)
    def _(t):
        for copy in incoming(t):
            copy.wait()
        rows = [[] for _ in range(4)]
        for j in tiles:
            s = lane_slice(j)
            rows[0].append(part_ref[t, 0, :, s] - flow_ref[0, :, s] * south_row_ref[t, :, s])
            rows[1].append(part_ref[t, 1, :, s])
            rows[2].append(part_ref[t, 2, :, s])
            gap = north_row_ref[t, :, s] - own_last_ref[t, :, s]
            rows[3].append(part_ref[t, 3, :, s] + flow_ref[1, :, s] * gap)
        for r in range(4):
            x = rows[r]
            e = east_tiles(x)
            w = west_tiles(x)
            for j in tiles:
                s = lane_slice(j)
                center = coef_ref[4, r, :, s] if r < 3 else center_ref[:, s]
                out = x[j] * center + e[j] * coef_ref[0, r, :, s] - w[j] * coef_ref[1, r, :, s]
                if r < 3:
                    out = out + rows[r + 1][j] * coef_ref[2, r, :, s]
                if r > 0:
                    out = out - rows[r - 1][j] * coef_ref[3, r, :, s]
                if r in (1, 2):
                    mid_ref[r - 1, t, :, s] = out
                else:
                    edge_ref[r // 3, t, :, s] = out
        for copy in outgoing(t):
            copy.start()

    for q in range(2):
        for j in tiles:
            s = lane_slice(j)
            inside = inside_ref[q, :, s]
            sum_out_ref[q, :, s] = level_sums([mid_ref[q, t, :, s] * inside for t in range(8)])

    @pl.loop(0, 8)
    def _(t):
        for copy in outgoing(t):
            copy.wait()

    flow_copy.wait()


def close_kernel(
    lev_ref, edge_hbm, flow_hbm, south_part_ref, north_part_ref, sum_mid_ref, band_ref, adv_ref, keep_ref, send_ref,
    edge_ref, flow_ref, inside_ref, sum_ref, sems,
):
    def incoming(t):
        return pltpu.make_async_copy(edge_hbm.at[:, t], edge_ref.at[:, t], sems.at[t])

    flow_copy = pltpu.make_async_copy(flow_hbm, flow_ref, sems.at[8])
    flow_copy.start()

    @pl.loop(0, 8)
    def _(t):
        incoming(t).start()

    for q in range(2):
        inside_ref[q] = inside_band(lev_ref, band_ref, 3 * q)
    sum_ref[1] = sum_mid_ref[0]
    sum_ref[2] = sum_mid_ref[1]
    flow_copy.wait()

    @pl.loop(0, 8)
    def _(t):
        incoming(t).wait()
        adv_ref[0, t] = edge_ref[0, t] - flow_ref[0] * south_part_ref[t]
        adv_ref[1, t] = edge_ref[1, t] + flow_ref[1] * north_part_ref[t]

    for q in range(2):
        for j in range(16):
            s = lane_slice(j)
            inside = inside_ref[q, :, s]
            sum_ref[3 * q, :, s] = level_sums([adv_ref[q, t, :, s] * inside for t in range(8)])

    core = lax.rem(lev_ref[0], 2)
    keep_ref[...] = sum_ref[pl.ds(2 * core, 2)]
    send_ref[...] = sum_ref[pl.ds(2 - 2 * core, 2)]


def halves_of(x):
    high = x.astype(jnp.bfloat16)
    return high, (x - high.astype(F32)).astype(jnp.bfloat16)


def column_kernel(lev_ref, band_ref, flux_ref, inv_ref, gain_ref, matrix_ref):
    lev = lev_ref[0]
    core = lax.rem(lev, 2)
    block = lax.div(lev, 2)
    wide = (64, 128)
    row_pick = (lax.broadcasted_iota(jnp.int32, (64, 8), 0) & 7) == lax.broadcasted_iota(jnp.int32, (64, 8), 1)
    lane = lax.broadcasted_iota(jnp.int32, (16, 128), 1)
    half = jnp.where(lane < 64, core, 1 - core)
    lane_pick = half * 8 + (lane & 7) == lax.broadcasted_iota(jnp.int32, (16, 128), 0)
    same_tracer = (lax.broadcasted_iota(jnp.int32, wide, 0) >> 3) == ((lax.broadcasted_iota(jnp.int32, wide, 1) & 63) >> 3)
    row_pick = jnp.where(row_pick, 1.0, 0.0).astype(F32)
    lane_pick = jnp.where(lane_pick, 1.0, 0.0).astype(F32)
    exact = dict(precision=lax.Precision.HIGHEST, preferred_element_type=F32)
    for r in range(4):
        first = band_ref[0, r : r + 1, :]
        last = band_ref[1, r : r + 1, :]
        scaled = flux_ref[r : r + 1, :] / (last - first).astype(F32)
        inv = inv_ref[r, block, pl.ds(pl.multiple_of(core * 8, 8), 8), :]
        gain = jnp.zeros((8, 2048), F32)
        for k in range(16):
            level_k = block * 16 + k
            weight = jnp.where((first <= level_k) & (level_k < last), scaled, 0.0)
            gain = gain + inv[:, k : k + 1] * weight
        gain_ref[r] = gain
        spread = lax.dot(lax.dot(row_pick, inv, **exact), lane_pick, **exact)
        high, low = halves_of(jnp.where(same_tracer, spread, 0.0))
        matrix_ref[r, 0:64, 0:128] = high
        matrix_ref[r, 0:64, 128:256] = high
        matrix_ref[r, 64:128, 0:128] = low
        matrix_ref[r, 64:128, 128:256] = jnp.zeros_like(low)


def diffuse_rows(rows, lev_ref, adv_ref, other_ref, band_ref, flux_ref, matrix_ref, out_ref, ready):
    lev = lev_ref[0]
    level = lax.broadcasted_iota(jnp.int32, (8, 2048), 0)
    own_level = level + lev * 8
    other_level = level + (lev + 1 - 2 * lax.rem(lev, 2)) * 8
    for q, r in enumerate(rows):
        first = band_ref[0, r : r + 1, :]
        last = band_ref[1, r : r + 1, :]
        flux = flux_ref[r : r + 1, :]

        def rest(values, levels):
            kept = 1.0 - jnp.where((levels >= first) & (levels < last), flux, 0.0)
            return halves_of((values * kept[None]).reshape(64, 2048))

        ready(q)
        own_high, own_low = rest(adv_ref[q], own_level)
        other_high, other_low = rest(other_ref[q], other_level)
        stacked = jnp.concatenate([own_high, other_high, own_low, other_low], axis=0)
        both = lax.dot(matrix_ref[r], stacked, preferred_element_type=F32)
        out_ref[q] = (both[:64] + both[64:]).reshape(8, 8, 2048)


def diffuse_mid_kernel(
    lev_ref, adv_hbm, other_hbm, band_ref, flux_ref, matrix_ref, out_hbm, adv_ref, other_ref, out_ref, sems
):
    copies = [
        [
            pltpu.make_async_copy(adv_hbm.at[q], adv_ref.at[q], sems.at[q, 0]),
            pltpu.make_async_copy(other_hbm.at[q], other_ref.at[q], sems.at[q, 1]),
        ]
        for q in range(2)
    ]
    for pair in copies:
        for copy in pair:
            copy.start()

    def ready(q):
        for copy in copies[q]:
            copy.wait()

    diffuse_rows((1, 2), lev_ref, adv_ref, other_ref, band_ref, flux_ref, matrix_ref, out_ref, ready)
    result = pltpu.make_async_copy(out_ref, out_hbm, sems.at[2, 0])
    result.start()
    result.wait()


def diffuse_edge_kernel(lev_ref, adv_ref, other_ref, band_ref, flux_ref, matrix_ref, out_ref):
    diffuse_rows((0, 3), lev_ref, adv_ref, other_ref, band_ref, flux_ref, matrix_ref, out_ref, lambda q: None)


def finish_kernel(
    lev_ref, mid_hbm, edge_ref, gain_ref, own_ref, other_ref, forcing_ref, out_ref, sum_ref, done_ref, mid_ref, sems, mid_sems
):
    def incoming(t):
        return pltpu.make_async_copy(mid_hbm.at[:, t], mid_ref.at[:, t], mid_sems.at[t])

    @pl.loop(0, 8)
    def _(t):
        incoming(t).start()

    core = lax.rem(lev_ref[0], 2)
    for q in range(2):
        for j in range(16):
            sum_ref[2 * core + q, j] = own_ref[q, :, lane_slice(j)]
            sum_ref[2 - 2 * core + q, j] = other_ref[q, :, lane_slice(j)]

    @pl.loop(0, 8)
    def _(t):
        incoming(t).wait()
        for k in range(8):
            tiles = []
            for j in (2 * k, 2 * k + 1):
                s = lane_slice(j)
                for r in range(4):
                    total = sum_ref[r, j, pl.ds(t, 8, stride=0), :]
                    forcing = forcing_ref[4 * r + j // 4, :, lane_slice(j % 4)]
                    base = mid_ref[r - 1, t, :, s] if r in (1, 2) else edge_ref[r // 3, t, :, s]
                    tiles.append(base + gain_ref[r, :, s] * total + forcing)
            tiles = swap_axes8(tiles)
            for level in range(8):
                done_ref[t, pl.ds(level * 64 + k * 8, 8), :] = tiles[level]
        pltpu.make_async_copy(done_ref.at[t], out_ref.at[t], sems.at[t]).start()

    @pl.loop(0, 8)
    def _(t):
        pltpu.make_async_copy(done_ref.at[t], out_ref.at[t], sems.at[t]).wait()


def pack_kernel(lat_ref, count_ref, values_ref, column_ref, out_ref, line_ref):
    lat = lat_ref[0]
    slot = lax.broadcasted_iota(jnp.int32, (16, LANES), 0)
    line_ref[...] = jnp.zeros((16, LANES), F32)
    line_ref[:, 0:16] = column_ref[...].astype(F32)
    placed = pltpu.roll(line_ref[...], lax.rem(lat, 8) * 16, 1)
    low = jnp.where(lat < 8, placed, 0.0)
    high = jnp.where(lat < 8, 0.0, placed)
    for d in range(16):
        out_ref[d, 0:16, :] = jnp.where(slot < count_ref[d], values_ref[d], 0.0)
        out_ref[d, 16:24, :] = jnp.zeros((8, LANES), F32)
        out_ref[d, 16:17, :] = low[d : d + 1]
        out_ref[d, 17:18, :] = high[d : d + 1]


def forcing_kernel(packed_ref, out_ref):
    lines = packed_ref[0, 16:18, :]
    for source in range(1, 16):
        lines = lines + packed_ref[source, 16:18, :]
    total = jnp.zeros((512, LANES), F32)
    column = lax.broadcasted_iota(jnp.int32, (512, LANES), 0).astype(F32)
    for part in range(2):
        hit = jnp.where(column == lines[part : part + 1], 1.0, 0.0).astype(F32)
        values = jnp.concatenate([packed_ref[8 * part + n, 0:16, :] for n in range(8)], axis=0)
        total = total + lax.dot(hit, values, precision=lax.Precision.HIGHEST, preferred_element_type=F32)
    out_ref[...] = total.T.reshape(16, 8, 512)


def body(adjoint_in, courant_lon, courant_lat, mass_flux, conv_band, diff_inverse, obs_values, obs_column, obs_count):
    tracers, levels, rows, lons = adjoint_in.shape
    lev = lax.axis_index("lev").astype(jnp.int32).reshape(1)
    lat = lax.axis_index("lat").astype(jnp.int32).reshape(1)
    lev_count = lax.axis_size("lev")
    lat_count = lax.axis_size("lat")
    smem = pl.BlockSpec(memory_space=pltpu.SMEM)
    shape = lambda *dims: jax.ShapeDtypeStruct(dims, F32)

    a_view = split_rows(adjoint_in).reshape(tracers, 512, LANES)
    u_view = split_rows(courant_lon).reshape(512, LANES)
    v_view = split_rows(courant_lat).reshape(512, LANES)

    vmem = pl.BlockSpec(memory_space=pltpu.VMEM)
    hbm = pl.BlockSpec(memory_space=pltpu.HBM)
    small = pltpu.CompilerParams(vmem_limit_bytes=16 << 20)
    row_scratch = pltpu.VMEM((4, 8, lons), F32)

    def far(*dims):
        return pltpu.HBM(dims, F32)

    def keep_far(x):
        return pltpu.with_memory_space_constraint(x, pltpu.HBM)

    last_row, first_row = pl.pallas_call(
        edge_kernel,
        in_specs=[hbm] * 2,
        out_specs=[hbm] * 2,
        out_shape=[far(8, 8, lons), far(9, 8, lons)],
        scratch_shapes=[
            pltpu.VMEM((8, 512, LANES), F32), pltpu.VMEM((512, LANES), F32), pltpu.VMEM((8, 8, lons), F32),
            pltpu.VMEM((9, 8, lons), F32), pltpu.SemaphoreType.DMA((9, 3)),
        ],
        compiler_params=small,
    )(keep_far(a_view), keep_far(v_view))
    part, to_north, to_south, coef = pl.pallas_call(
        prep_kernel,
        in_specs=[hbm] * 3,
        out_specs=[hbm] * 4,
        out_shape=[far(8, 4, 8, lons), far(8, 8, lons), far(8, 8, lons), far(5, 4, 8, lons)],
        scratch_shapes=[
            pltpu.VMEM((8, 512, LANES), F32), pltpu.VMEM((512, LANES), F32), pltpu.VMEM((512, LANES), F32),
            row_scratch, row_scratch, pltpu.VMEM((8, 4, 8, lons), F32), pltpu.VMEM((5, 4, 8, lons), F32),
            pltpu.SemaphoreType.DMA((9, 4)),
        ],
        compiler_params=small,
    )(keep_far(a_view), keep_far(u_view), keep_far(v_view))
    north = [(i, i + 1) for i in range(lat_count - 1)]
    south = [(i + 1, i) for i in range(lat_count - 1)]
    south_row = lax.ppermute(last_row, "lat", north)
    north_row = lax.ppermute(first_row, "lat", south)
    south_part = lax.ppermute(to_north, "lat", north)
    north_part = lax.ppermute(to_south, "lat", south)

    packed = pl.pallas_call(
        pack_kernel,
        in_specs=[smem, smem, vmem, vmem],
        out_specs=vmem,
        out_shape=shape(16, 24, LANES),
        scratch_shapes=[pltpu.VMEM((16, LANES), F32)],
        compiler_params=small,
    )(lat, obs_count.reshape(16), obs_values.reshape(16, 16, LANES), obs_column.reshape(16, 16))
    packed = lax.all_to_all(packed, "lat", split_axis=0, concat_axis=0, tiled=True)

    forcing = pl.pallas_call(
        forcing_kernel, in_specs=[vmem], out_specs=vmem, out_shape=shape(16, 8, 512), compiler_params=small
    )(packed)
    forcing = lax.all_to_all(forcing, "lev", split_axis=0, concat_axis=0, tiled=True)

    gain, matrix = pl.pallas_call(
        column_kernel,
        in_specs=[smem] + [vmem] * 3,
        out_specs=[vmem] * 2,
        out_shape=[shape(4, 8, lons), jax.ShapeDtypeStruct((4, 128, 256), jnp.bfloat16)],
        compiler_params=small,
    )(lev, conv_band, mass_flux, diff_inverse)

    two_rows = pltpu.VMEM((2, 8, 8, lons), F32)
    one_row = pltpu.VMEM((2, 8, lons), F32)
    swap = [(i, i ^ 1) for i in range(lev_count)]
    mid, edge, flow, sum_mid = pl.pallas_call(
        mid_kernel,
        in_specs=[smem] + [hbm] * 2 + [vmem] * 2 + [hbm, vmem],
        out_specs=[hbm] * 3 + [vmem],
        out_shape=[far(2, 8, 8, lons), far(2, 8, 8, lons), far(2, 8, lons), shape(2, 8, lons)],
        scratch_shapes=[
            pltpu.VMEM((8, 4, 8, lons), F32), pltpu.VMEM((8, 8, lons), F32), pltpu.VMEM((5, 4, 8, lons), F32),
            one_row, pltpu.VMEM((8, lons), F32), one_row, two_rows, two_rows, pltpu.SemaphoreType.DMA((9, 4)),
        ],
        compiler_params=small,
    )(lev, keep_far(part), keep_far(last_row), south_row, north_row, keep_far(coef), conv_band)
    mid_other = lax.ppermute(mid, "lev", swap)
    base_mid = pl.pallas_call(
        diffuse_mid_kernel,
        in_specs=[smem] + [hbm] * 2 + [vmem] * 3,
        out_specs=hbm,
        out_shape=far(2, 8, 8, lons),
        scratch_shapes=[two_rows] * 3 + [pltpu.SemaphoreType.DMA((3, 2))],
        compiler_params=small,
    )(lev, keep_far(mid), mid_other, conv_band, mass_flux, matrix)

    adv, keep, send = pl.pallas_call(
        close_kernel,
        in_specs=[smem] + [hbm] * 2 + [vmem] * 4,
        out_specs=[vmem] * 3,
        out_shape=[shape(2, 8, 8, lons), shape(2, 8, lons), shape(2, 8, lons)],
        scratch_shapes=[two_rows, one_row, one_row, row_scratch, pltpu.SemaphoreType.DMA((9,))],
        compiler_params=small,
    )(lev, keep_far(edge), keep_far(flow), south_part, north_part, sum_mid, conv_band)

    swapped = lax.ppermute(send, "lev", swap)
    chip_sum = keep + swapped
    blocks = lev_count // 2
    lines = blocks // 2 - 1
    moved = []
    for shift in range(1, lines):
        pairs = []
        for y in range(lines):
            for n in range(4):
                pairs.append((4 * (y + 1) + n, 4 * ((y + shift) % lines + 1) + n))
        moved.append(lax.ppermute(chip_sum, "lev", pairs))
    total = sum(moved, chip_sum)
    adv_other = lax.ppermute(adv, "lev", swap)
    pairs = [(2 * n + c, 2 * (n ^ 1) + c) for n in range(2, blocks) for c in range(2)]
    total = total + lax.ppermute(total, "lev", pairs)
    total_other = lax.ppermute(total, "lev", swap)

    base_edge = pl.pallas_call(
        diffuse_edge_kernel,
        in_specs=[smem] + [vmem] * 5,
        out_specs=vmem,
        out_shape=shape(2, 8, 8, lons),
        compiler_params=small,
    )(lev, adv, adv_other, conv_band, mass_flux, matrix)

    out = pl.pallas_call(
        finish_kernel,
        in_specs=[smem, hbm] + [vmem] * 5,
        out_specs=hbm,
        out_shape=shape(tracers, 512, LANES),
        scratch_shapes=[
            pltpu.VMEM((4, 16, 8, LANES), F32), pltpu.VMEM((8, 512, LANES), F32), two_rows,
            pltpu.SemaphoreType.DMA((8,)), pltpu.SemaphoreType.DMA((8,)),
        ],
        compiler_params=small,
    )(lev, keep_far(base_mid), base_edge, gain, total, total_other, forcing)
    return join_rows(out.reshape(tracers, levels, 64, LANES), rows, lons)


def solution(mesh):
    placed = (
        P(None, "lev", "lat", None),
        P("lev", "lat", None),
        P("lev", "lat", None),
        P("lat", None),
        P(None, "lat", None),
        P("lat", None, None, None),
        P("lev", "lat", None, None, None),
        P("lev", "lat", None, None),
        P("lev", "lat", None),
    )

    def step(*args):
        return body(*args)

    step = jax.shard_map(
        step, mesh=mesh, in_specs=placed, out_specs=P(None, "lev", "lat", None), check_vma=False
    )
    return step
```

```python
import jax
import jax.numpy as jnp
from jax import lax
from jax.experimental import pallas as pl
from jax.experimental.pallas import tpu as pltpu
from jax.sharding import PartitionSpec as P


F32 = jnp.float32
LANES = 128


def split_rows(x):
    lead = x.shape[:-2]
    rows, lons = x.shape[-2:]
    x = x.reshape(*lead, rows, lons // LANES, LANES).swapaxes(-3, -2)
    return x.reshape(*lead, rows * lons // LANES, LANES)


def join_rows(x, rows, lons):
    lead = x.shape[:-2]
    x = x.reshape(*lead, lons // LANES, rows, LANES).swapaxes(-3, -2)
    return x.reshape(*lead, rows, lons)


def lane_slice(j):
    return pl.ds(j * LANES, LANES)


def swap_axes8(tiles):
    row = lax.broadcasted_iota(jnp.int32, (8, LANES), 0)
    tiles = list(tiles)
    for step in (4, 2, 1):
        low_half = (row & step) == 0
        for i in range(8):
            if i & step == 0:
                low, high = tiles[i], tiles[i + step]
                tiles[i] = jnp.where(low_half, low, pltpu.roll(high, step, 0))
                tiles[i + step] = jnp.where(low_half, pltpu.roll(low, 8 - step, 0), high)
    return tiles


def level_sums(tiles):
    row = lax.broadcasted_iota(jnp.int32, (8, LANES), 0)
    for step in (1, 2, 4):
        low = (row & step) == 0
        tiles = [
            jnp.where(low, a, b) + pltpu.roll(jnp.where(low, b, a), step, 0) for a, b in zip(tiles[::2], tiles[1::2])
        ]
    return tiles[0]


def unpack_rows(source, target):
    for k in range(8):
        tiles = swap_axes8([source(level * 64 + k * 8) for level in range(8)])
        for half in range(2):
            for r in range(4):
                target[r, :, lane_slice(2 * k + half)] = tiles[4 * half + r]


def east_tiles(tiles):
    lane = lax.broadcasted_iota(jnp.int32, tiles[0].shape, 1)
    turned = [pltpu.roll(x, LANES - 1, 1) for x in tiles]
    count = len(tiles)
    return [jnp.where(lane == LANES - 1, turned[(j + 1) % count], turned[j]) for j in range(count)]


def west_tiles(tiles):
    lane = lax.broadcasted_iota(jnp.int32, tiles[0].shape, 1)
    turned = [pltpu.roll(x, 1, 1) for x in tiles]
    return [jnp.where(lane == 0, turned[j - 1], turned[j]) for j in range(len(tiles))]


def flow_coefficients(u_ref, v_ref, u_rows, v_rows, coef_ref):
    unpack_rows(lambda start: u_ref[pl.ds(start, 8), :], u_rows)
    unpack_rows(lambda start: v_ref[pl.ds(start, 8), :], v_rows)
    for r in range(4):
        u = [u_rows[r, :, lane_slice(j)] for j in range(16)]
        ue = east_tiles(u)
        for j in range(16):
            s = lane_slice(j)
            east = jnp.maximum(ue[j], 0.0)
            west = jnp.minimum(u[j], 0.0)
            south = jnp.minimum(v_rows[r, :, s], 0.0)
            center = 1.0 - east + west + south
            if r < 3:
                north = jnp.maximum(v_rows[r + 1, :, s], 0.0)
                center = center - north
                coef_ref[2, r, :, s] = north
            coef_ref[0, r, :, s] = east
            coef_ref[1, r, :, s] = west
            coef_ref[3, r, :, s] = south
            coef_ref[4, r, :, s] = center


def edge_kernel(a_hbm, v_hbm, last_hbm, first_hbm, a_ref, v_ref, last_ref, first_ref, sems):
    def incoming(t):
        return pltpu.make_async_copy(a_hbm.at[t], a_ref.at[t], sems.at[t, 0])

    def outgoing(t):
        return [
            pltpu.make_async_copy(last_ref.at[t], last_hbm.at[t], sems.at[t, 1]),
            pltpu.make_async_copy(first_ref.at[t], first_hbm.at[t], sems.at[t, 2]),
        ]

    faces_in = pltpu.make_async_copy(v_hbm, v_ref, sems.at[8, 0])
    faces_out = pltpu.make_async_copy(first_ref.at[8], first_hbm.at[8], sems.at[8, 1])
    faces_in.start()

    @pl.loop(0, 8)
    def _(t):
        incoming(t).start()

    faces_in.wait()
    for k in range(8):
        tiles = swap_axes8([v_ref[pl.ds(level * 64 + k * 8, 8), :] for level in range(8)])
        for half in range(2):
            first_ref[8, :, lane_slice(2 * k + half)] = tiles[4 * half]
    faces_out.start()

    @pl.loop(0, 8)
    def _(t):
        incoming(t).wait()
        for k in range(8):
            tiles = swap_axes8([a_ref[t, pl.ds(level * 64 + k * 8, 8), :] for level in range(8)])
            for half in range(2):
                first_ref[t, :, lane_slice(2 * k + half)] = tiles[4 * half]
                last_ref[t, :, lane_slice(2 * k + half)] = tiles[4 * half + 3]
        for copy in outgoing(t):
            copy.start()

    @pl.loop(0, 8)
    def _(t):
        for copy in outgoing(t):
            copy.wait()

    faces_out.wait()


def prep_kernel(
    a_hbm, u_hbm, v_hbm, part_hbm, north_hbm, south_hbm, coef_hbm,
    a_ref, u_ref, v_ref, rows_ref, v_rows, part_ref, coef_ref, sems,
):
    faces = [
        pltpu.make_async_copy(u_hbm, u_ref, sems.at[8, 2]),
        pltpu.make_async_copy(v_hbm, v_ref, sems.at[8, 3]),
    ]
    for copy in faces:
        copy.start()

    def incoming(t):
        return pltpu.make_async_copy(a_hbm.at[t], a_ref.at[t], sems.at[t, 3])

    @pl.loop(0, 8)
    def _(t):
        incoming(t).start()

    def copies(t):
        return [
            pltpu.make_async_copy(part_ref.at[t], part_hbm.at[t], sems.at[t, 0]),
            pltpu.make_async_copy(part_ref.at[t, 3], north_hbm.at[t], sems.at[t, 1]),
            pltpu.make_async_copy(part_ref.at[t, 0], south_hbm.at[t], sems.at[t, 2]),
        ]

    for copy in faces:
        copy.wait()
    flow_coefficients(u_ref, v_ref, rows_ref, v_rows, coef_ref)
    coef_copy = pltpu.make_async_copy(coef_ref, coef_hbm, sems.at[8, 0])
    coef_copy.start()

    @pl.loop(0, 8)
    def _(t):
        incoming(t).wait()
        unpack_rows(lambda start: a_ref[t, pl.ds(start, 8), :], rows_ref)
        for r in range(4):
            row = [rows_ref[r, :, lane_slice(j)] for j in range(16)]
            e = east_tiles(row)
            w = west_tiles(row)
            for j in range(16):
                s = lane_slice(j)
                out = row[j] * coef_ref[4, r, :, s] + e[j] * coef_ref[0, r, :, s] - w[j] * coef_ref[1, r, :, s]
                if r < 3:
                    out = out + rows_ref[r + 1, :, s] * coef_ref[2, r, :, s]
                if r > 0:
                    out = out - rows_ref[r - 1, :, s] * coef_ref[3, r, :, s]
                part_ref[t, r, :, s] = out
        for copy in copies(t):
            copy.start()

    @pl.loop(0, 8)
    def _(t):
        for copy in copies(t):
            copy.wait()

    coef_copy.wait()


def inside_band(lev_ref, band_ref, r):
    level = lax.broadcasted_iota(jnp.int32, (8, 2048), 0) + lev_ref[0] * 8
    first = band_ref[0, r : r + 1, :]
    last = band_ref[1, r : r + 1, :]
    return jnp.where((level >= first) & (level < last), 1.0, 0.0).astype(F32)


def mid_kernel(
    lev_ref, part_hbm, own_last_hbm, south_row_ref, north_row_ref, coef_hbm, band_ref,
    mid_hbm, edge_hbm, flow_hbm, keep_ref, send_ref,
    part_ref, own_last_ref, coef_ref, flow_ref, center_ref, inside_ref, mid_ref, edge_ref, sum_ref, sems,
):
    tiles = range(16)

    def incoming(t):
        return [
            pltpu.make_async_copy(part_hbm.at[t], part_ref.at[t], sems.at[t, 0]),
            pltpu.make_async_copy(own_last_hbm.at[t], own_last_ref.at[t], sems.at[t, 1]),
        ]

    def outgoing(t):
        return [
            pltpu.make_async_copy(mid_ref.at[:, t], mid_hbm.at[:, t], sems.at[t, 2]),
            pltpu.make_async_copy(edge_ref.at[:, t], edge_hbm.at[:, t], sems.at[t, 3]),
        ]

    coef_copy = pltpu.make_async_copy(coef_hbm, coef_ref, sems.at[8, 0])
    flow_copy = pltpu.make_async_copy(flow_ref, flow_hbm, sems.at[8, 1])
    coef_copy.start()

    @pl.loop(0, 8)
    def _(t):
        for copy in incoming(t):
            copy.start()

    for q in range(2):
        inside_ref[q] = inside_band(lev_ref, band_ref, q + 1)
    coef_copy.wait()
    north = jnp.maximum(north_row_ref[8], 0.0)
    flow_ref[0] = coef_ref[3, 0]
    flow_ref[1] = north
    center_ref[...] = coef_ref[4, 3] - north
    flow_copy.start()

    @pl.loop(0, 8)
    def _(t):
        for copy in incoming(t):
            copy.wait()
        rows = [[] for _ in range(4)]
        for j in tiles:
            s = lane_slice(j)
            rows[0].append(part_ref[t, 0, :, s] - flow_ref[0, :, s] * south_row_ref[t, :, s])
            rows[1].append(part_ref[t, 1, :, s])
            rows[2].append(part_ref[t, 2, :, s])
            gap = north_row_ref[t, :, s] - own_last_ref[t, :, s]
            rows[3].append(part_ref[t, 3, :, s] + flow_ref[1, :, s] * gap)
        for r in range(4):
            x = rows[r]
            e = east_tiles(x)
            w = west_tiles(x)
            for j in tiles:
                s = lane_slice(j)
                center = coef_ref[4, r, :, s] if r < 3 else center_ref[:, s]
                out = x[j] * center + e[j] * coef_ref[0, r, :, s] - w[j] * coef_ref[1, r, :, s]
                if r < 3:
                    out = out + rows[r + 1][j] * coef_ref[2, r, :, s]
                if r > 0:
                    out = out - rows[r - 1][j] * coef_ref[3, r, :, s]
                if r in (1, 2):
                    mid_ref[r - 1, t, :, s] = out
                else:
                    edge_ref[r // 3, t, :, s] = out
        for copy in outgoing(t):
            copy.start()

    for q in range(2):
        for j in tiles:
            s = lane_slice(j)
            inside = inside_ref[q, :, s]
            sum_ref[q, :, s] = level_sums([mid_ref[q, t, :, s] * inside for t in range(8)])

    core = lax.rem(lev_ref[0], 2)
    keep_ref[...] = sum_ref[pl.ds(core, 1)]
    send_ref[...] = sum_ref[pl.ds(1 - core, 1)]

    @pl.loop(0, 8)
    def _(t):
        for copy in outgoing(t):
            copy.wait()

    flow_copy.wait()


def close_kernel(
    lev_ref, edge_hbm, flow_hbm, south_part_hbm, north_part_hbm, band_ref, adv_ref, keep_ref, send_ref,
    edge_ref, south_part_ref, north_part_ref, flow_ref, inside_ref, sum_ref, sems,
):
    def incoming(t):
        return [
            pltpu.make_async_copy(edge_hbm.at[:, t], edge_ref.at[:, t], sems.at[t, 0]),
            pltpu.make_async_copy(south_part_hbm.at[t], south_part_ref.at[t], sems.at[t, 1]),
            pltpu.make_async_copy(north_part_hbm.at[t], north_part_ref.at[t], sems.at[t, 2]),
        ]

    flow_copy = pltpu.make_async_copy(flow_hbm, flow_ref, sems.at[8, 0])
    flow_copy.start()

    @pl.loop(0, 8)
    def _(t):
        for copy in incoming(t):
            copy.start()

    for q in range(2):
        inside_ref[q] = inside_band(lev_ref, band_ref, 3 * q)
    flow_copy.wait()

    @pl.loop(0, 8)
    def _(t):
        for copy in incoming(t):
            copy.wait()
        adv_ref[0, t] = edge_ref[0, t] - flow_ref[0] * south_part_ref[t]
        adv_ref[1, t] = edge_ref[1, t] + flow_ref[1] * north_part_ref[t]

    for q in range(2):
        for j in range(16):
            s = lane_slice(j)
            inside = inside_ref[q, :, s]
            sum_ref[q, :, s] = level_sums([adv_ref[q, t, :, s] * inside for t in range(8)])

    core = lax.rem(lev_ref[0], 2)
    keep_ref[...] = sum_ref[pl.ds(core, 1)]
    send_ref[...] = sum_ref[pl.ds(1 - core, 1)]


def halves_of(x):
    high = x.astype(jnp.bfloat16)
    return high, (x - high.astype(F32)).astype(jnp.bfloat16)


def column_kernel(lev_ref, band_ref, flux_ref, inv_ref, gain_ref, matrix_ref):
    lev = lev_ref[0]
    core = lax.rem(lev, 2)
    block = lax.div(lev, 2)
    wide = (64, 128)
    row_pick = (lax.broadcasted_iota(jnp.int32, (64, 8), 0) & 7) == lax.broadcasted_iota(jnp.int32, (64, 8), 1)
    lane = lax.broadcasted_iota(jnp.int32, (16, 128), 1)
    half = jnp.where(lane < 64, core, 1 - core)
    lane_pick = half * 8 + (lane & 7) == lax.broadcasted_iota(jnp.int32, (16, 128), 0)
    same_tracer = (lax.broadcasted_iota(jnp.int32, wide, 0) >> 3) == ((lax.broadcasted_iota(jnp.int32, wide, 1) & 63) >> 3)
    row_pick = jnp.where(row_pick, 1.0, 0.0).astype(F32)
    lane_pick = jnp.where(lane_pick, 1.0, 0.0).astype(F32)
    exact = dict(precision=lax.Precision.HIGHEST, preferred_element_type=F32)
    for r in range(4):
        first = band_ref[0, r : r + 1, :]
        last = band_ref[1, r : r + 1, :]
        scaled = flux_ref[r : r + 1, :] / (last - first).astype(F32)
        inv = inv_ref[r, block, pl.ds(pl.multiple_of(core * 8, 8), 8), :]
        gain = jnp.zeros((8, 2048), F32)
        for k in range(16):
            level_k = block * 16 + k
            weight = jnp.where((first <= level_k) & (level_k < last), scaled, 0.0)
            gain = gain + inv[:, k : k + 1] * weight
        gain_ref[r] = gain
        spread = lax.dot(lax.dot(row_pick, inv, **exact), lane_pick, **exact)
        high, low = halves_of(jnp.where(same_tracer, spread, 0.0))
        matrix_ref[r, 0:64, 0:128] = high
        matrix_ref[r, 0:64, 128:256] = high
        matrix_ref[r, 64:128, 0:128] = low
        matrix_ref[r, 64:128, 128:256] = jnp.zeros_like(low)


def diffuse_rows(rows, lev_ref, adv_ref, other_ref, band_ref, flux_ref, matrix_ref, out_ref, ready):
    lev = lev_ref[0]
    level = lax.broadcasted_iota(jnp.int32, (8, 2048), 0)
    own_level = level + lev * 8
    other_level = level + (lev + 1 - 2 * lax.rem(lev, 2)) * 8
    for q, r in enumerate(rows):
        first = band_ref[0, r : r + 1, :]
        last = band_ref[1, r : r + 1, :]
        flux = flux_ref[r : r + 1, :]

        def rest(values, levels):
            kept = 1.0 - jnp.where((levels >= first) & (levels < last), flux, 0.0)
            return halves_of((values * kept[None]).reshape(64, 2048))

        ready(q)
        own_high, own_low = rest(adv_ref[q], own_level)
        other_high, other_low = rest(other_ref[q], other_level)
        stacked = jnp.concatenate([own_high, other_high, own_low, other_low], axis=0)
        both = lax.dot(matrix_ref[r], stacked, preferred_element_type=F32)
        out_ref[q] = (both[:64] + both[64:]).reshape(8, 8, 2048)


def diffuse_mid_kernel(
    lev_ref, adv_hbm, other_hbm, band_ref, flux_ref, matrix_ref, out_ref, adv_ref, other_ref, sems
):
    copies = [
        [
            pltpu.make_async_copy(adv_hbm.at[q], adv_ref.at[q], sems.at[q, 0]),
            pltpu.make_async_copy(other_hbm.at[q], other_ref.at[q], sems.at[q, 1]),
        ]
        for q in range(2)
    ]
    for pair in copies:
        for copy in pair:
            copy.start()

    def ready(q):
        for copy in copies[q]:
            copy.wait()

    diffuse_rows((1, 2), lev_ref, adv_ref, other_ref, band_ref, flux_ref, matrix_ref, out_ref, ready)


def diffuse_edge_kernel(lev_ref, adv_ref, other_ref, band_ref, flux_ref, matrix_ref, out_ref):
    diffuse_rows((0, 3), lev_ref, adv_ref, other_ref, band_ref, flux_ref, matrix_ref, out_ref, lambda q: None)


def finish_kernel(lev_ref, mid_ref, edge_ref, gain_ref, own_ref, other_ref, forcing_ref, out_ref, sum_ref, done_ref, sems):
    core = lax.rem(lev_ref[0], 2)
    for j in range(16):
        s = lane_slice(j)
        sum_ref[1 + core, j] = own_ref[0, :, s]
        sum_ref[3 * core, j] = own_ref[1, :, s]
        sum_ref[2 - core, j] = other_ref[0, :, s]
        sum_ref[3 - 3 * core, j] = other_ref[1, :, s]

    @pl.loop(0, 8)
    def _(t):
        for k in range(8):
            tiles = []
            for j in (2 * k, 2 * k + 1):
                s = lane_slice(j)
                for r in range(4):
                    total = sum_ref[r, j, pl.ds(t, 8, stride=0), :]
                    forcing = forcing_ref[4 * r + j // 4, :, lane_slice(j % 4)]
                    base = mid_ref[r - 1, t, :, s] if r in (1, 2) else edge_ref[r // 3, t, :, s]
                    tiles.append(base + gain_ref[r, :, s] * total + forcing)
            tiles = swap_axes8(tiles)
            for level in range(8):
                done_ref[t, pl.ds(level * 64 + k * 8, 8), :] = tiles[level]
        pltpu.make_async_copy(done_ref.at[t], out_ref.at[t], sems.at[t]).start()

    @pl.loop(0, 8)
    def _(t):
        pltpu.make_async_copy(done_ref.at[t], out_ref.at[t], sems.at[t]).wait()


def pack_kernel(lat_ref, count_ref, values_ref, column_ref, out_ref, line_ref):
    lat = lat_ref[0]
    slot = lax.broadcasted_iota(jnp.int32, (16, LANES), 0)
    line_ref[...] = jnp.zeros((16, LANES), F32)
    line_ref[:, 0:16] = column_ref[...].astype(F32)
    placed = pltpu.roll(line_ref[...], lax.rem(lat, 8) * 16, 1)
    low = jnp.where(lat < 8, placed, 0.0)
    high = jnp.where(lat < 8, 0.0, placed)
    for d in range(16):
        out_ref[d, 0:16, :] = jnp.where(slot < count_ref[d], values_ref[d], 0.0)
        out_ref[d, 16:24, :] = jnp.zeros((8, LANES), F32)
        out_ref[d, 16:17, :] = low[d : d + 1]
        out_ref[d, 17:18, :] = high[d : d + 1]


def forcing_kernel(packed_ref, out_ref):
    lines = packed_ref[0, 16:18, :]
    for source in range(1, 16):
        lines = lines + packed_ref[source, 16:18, :]
    total = jnp.zeros((512, LANES), F32)
    column = lax.broadcasted_iota(jnp.int32, (512, LANES), 0).astype(F32)
    for part in range(2):
        hit = jnp.where(column == lines[part : part + 1], 1.0, 0.0).astype(F32)
        values = jnp.concatenate([packed_ref[8 * part + n, 0:16, :] for n in range(8)], axis=0)
        total = total + lax.dot(hit, values, precision=lax.Precision.HIGHEST, preferred_element_type=F32)
    out_ref[...] = total.T.reshape(16, 8, 512)


def body(adjoint_in, courant_lon, courant_lat, mass_flux, conv_band, diff_inverse, obs_values, obs_column, obs_count):
    tracers, levels, rows, lons = adjoint_in.shape
    lev = lax.axis_index("lev").astype(jnp.int32).reshape(1)
    lat = lax.axis_index("lat").astype(jnp.int32).reshape(1)
    lev_count = lax.axis_size("lev")
    lat_count = lax.axis_size("lat")
    smem = pl.BlockSpec(memory_space=pltpu.SMEM)
    shape = lambda *dims: jax.ShapeDtypeStruct(dims, F32)

    a_view = split_rows(adjoint_in).reshape(tracers, 512, LANES)
    u_view = split_rows(courant_lon).reshape(512, LANES)
    v_view = split_rows(courant_lat).reshape(512, LANES)

    vmem = pl.BlockSpec(memory_space=pltpu.VMEM)
    hbm = pl.BlockSpec(memory_space=pltpu.HBM)
    small = pltpu.CompilerParams(vmem_limit_bytes=16 << 20)
    row_scratch = pltpu.VMEM((4, 8, lons), F32)

    def far(*dims):
        return pltpu.HBM(dims, F32)

    def keep_far(x):
        return pltpu.with_memory_space_constraint(x, pltpu.HBM)

    last_row, first_row = pl.pallas_call(
        edge_kernel,
        in_specs=[hbm] * 2,
        out_specs=[hbm] * 2,
        out_shape=[far(8, 8, lons), far(9, 8, lons)],
        scratch_shapes=[
            pltpu.VMEM((8, 512, LANES), F32), pltpu.VMEM((512, LANES), F32), pltpu.VMEM((8, 8, lons), F32),
            pltpu.VMEM((9, 8, lons), F32), pltpu.SemaphoreType.DMA((9, 3)),
        ],
        compiler_params=small,
    )(keep_far(a_view), keep_far(v_view))
    part, to_north, to_south, coef = pl.pallas_call(
        prep_kernel,
        in_specs=[hbm] * 3,
        out_specs=[hbm] * 4,
        out_shape=[far(8, 4, 8, lons), far(8, 8, lons), far(8, 8, lons), far(5, 4, 8, lons)],
        scratch_shapes=[
            pltpu.VMEM((8, 512, LANES), F32), pltpu.VMEM((512, LANES), F32), pltpu.VMEM((512, LANES), F32),
            row_scratch, row_scratch, pltpu.VMEM((8, 4, 8, lons), F32), pltpu.VMEM((5, 4, 8, lons), F32),
            pltpu.SemaphoreType.DMA((9, 4)),
        ],
        compiler_params=small,
    )(keep_far(a_view), keep_far(u_view), keep_far(v_view))
    north = [(i, i + 1) for i in range(lat_count - 1)]
    south = [(i + 1, i) for i in range(lat_count - 1)]
    south_row = lax.ppermute(last_row, "lat", north)
    north_row = lax.ppermute(first_row, "lat", south)
    south_part = lax.ppermute(to_north, "lat", north)
    north_part = lax.ppermute(to_south, "lat", south)

    packed = pl.pallas_call(
        pack_kernel,
        in_specs=[smem, smem, vmem, vmem],
        out_specs=vmem,
        out_shape=shape(16, 24, LANES),
        scratch_shapes=[pltpu.VMEM((16, LANES), F32)],
        compiler_params=small,
    )(lat, obs_count.reshape(16), obs_values.reshape(16, 16, LANES), obs_column.reshape(16, 16))
    packed = lax.all_to_all(packed, "lat", split_axis=0, concat_axis=0, tiled=True)

    forcing = pl.pallas_call(
        forcing_kernel, in_specs=[vmem], out_specs=vmem, out_shape=shape(16, 8, 512), compiler_params=small
    )(packed)
    forcing = lax.all_to_all(forcing, "lev", split_axis=0, concat_axis=0, tiled=True)

    gain, matrix = pl.pallas_call(
        column_kernel,
        in_specs=[smem] + [vmem] * 3,
        out_specs=[vmem] * 2,
        out_shape=[shape(4, 8, lons), jax.ShapeDtypeStruct((4, 128, 256), jnp.bfloat16)],
        compiler_params=small,
    )(lev, conv_band, mass_flux, diff_inverse)

    two_rows = pltpu.VMEM((2, 8, 8, lons), F32)
    one_row = pltpu.VMEM((2, 8, lons), F32)
    swap = [(i, i ^ 1) for i in range(lev_count)]
    mid, edge, flow, keep_mid, send_mid = pl.pallas_call(
        mid_kernel,
        in_specs=[smem] + [hbm] * 2 + [vmem] * 2 + [hbm, vmem],
        out_specs=[hbm] * 3 + [vmem] * 2,
        out_shape=[
            far(2, 8, 8, lons), far(2, 8, 8, lons), far(2, 8, lons), shape(1, 8, lons), shape(1, 8, lons)
        ],
        scratch_shapes=[
            pltpu.VMEM((8, 4, 8, lons), F32), pltpu.VMEM((8, 8, lons), F32), pltpu.VMEM((5, 4, 8, lons), F32),
            one_row, pltpu.VMEM((8, lons), F32), one_row, two_rows, two_rows, one_row, pltpu.SemaphoreType.DMA((9, 4)),
        ],
        compiler_params=small,
    )(lev, keep_far(part), keep_far(last_row), south_row, north_row, keep_far(coef), conv_band)

    blocks = lev_count // 2
    lines = blocks // 2 - 1

    def summed(keep, send):
        part_sum = keep + lax.ppermute(send, "lev", swap)
        moved = []
        for shift in range(1, lines):
            pairs = []
            for y in range(lines):
                for n in range(4):
                    pairs.append((4 * (y + 1) + n, 4 * ((y + shift) % lines + 1) + n))
            moved.append(lax.ppermute(part_sum, "lev", pairs))
        return sum(moved, part_sum)

    total_mid = summed(keep_mid, send_mid)

    adv, keep, send = pl.pallas_call(
        close_kernel,
        in_specs=[smem] + [hbm] * 4 + [vmem],
        out_specs=[vmem] * 3,
        out_shape=[shape(2, 8, 8, lons), shape(1, 8, lons), shape(1, 8, lons)],
        scratch_shapes=[
            two_rows, pltpu.VMEM((8, 8, lons), F32), pltpu.VMEM((8, 8, lons), F32), one_row, one_row, one_row,
            pltpu.SemaphoreType.DMA((9, 3)),
        ],
        compiler_params=small,
    )(lev, keep_far(edge), keep_far(flow), south_part, north_part, conv_band)
    total_edge = summed(keep, send)
    adv_other = lax.ppermute(adv, "lev", swap)
    mid_other = lax.ppermute(mid, "lev", swap)
    pairs = [(2 * n + c, 2 * (n ^ 1) + c) for n in range(2, blocks) for c in range(2)]
    total = jnp.concatenate([total_mid, total_edge], axis=0)
    total = total + lax.ppermute(total, "lev", pairs)
    total_other = lax.ppermute(total, "lev", swap)
    base_mid = pl.pallas_call(
        diffuse_mid_kernel,
        in_specs=[smem] + [hbm] * 2 + [vmem] * 3,
        out_specs=vmem,
        out_shape=shape(2, 8, 8, lons),
        scratch_shapes=[two_rows] * 2 + [pltpu.SemaphoreType.DMA((2, 2))],
        compiler_params=small,
    )(lev, keep_far(mid), mid_other, conv_band, mass_flux, matrix)
    base_edge = pl.pallas_call(
        diffuse_edge_kernel,
        in_specs=[smem] + [vmem] * 5,
        out_specs=vmem,
        out_shape=shape(2, 8, 8, lons),
        compiler_params=small,
    )(lev, adv, adv_other, conv_band, mass_flux, matrix)

    out = pl.pallas_call(
        finish_kernel,
        in_specs=[smem] + [vmem] * 6,
        out_specs=hbm,
        out_shape=shape(tracers, 512, LANES),
        scratch_shapes=[
            pltpu.VMEM((4, 16, 8, LANES), F32), pltpu.VMEM((8, 512, LANES), F32), pltpu.SemaphoreType.DMA((8,))
        ],
        compiler_params=small,
    )(lev, base_mid, base_edge, gain, total, total_other, forcing)
    return join_rows(out.reshape(tracers, levels, 64, LANES), rows, lons)


def solution(mesh):
    placed = (
        P(None, "lev", "lat", None),
        P("lev", "lat", None),
        P("lev", "lat", None),
        P("lat", None),
        P(None, "lat", None),
        P("lat", None, None, None),
        P("lev", "lat", None, None, None),
        P("lev", "lat", None, None),
        P("lev", "lat", None),
    )

    def step(*args):
        return body(*args)

    step = jax.shard_map(
        step, mesh=mesh, in_specs=placed, out_specs=P(None, "lev", "lat", None), check_vma=False
    )
    return step
```

```python
import jax
import jax.numpy as jnp
from jax import lax
from jax.experimental import pallas as pl
from jax.experimental.pallas import tpu as pltpu
from jax.sharding import PartitionSpec as P


F32 = jnp.float32
LANES = 128


def split_rows(x):
    lead = x.shape[:-2]
    rows, lons = x.shape[-2:]
    x = x.reshape(*lead, rows, lons // LANES, LANES).swapaxes(-3, -2)
    return x.reshape(*lead, rows * lons // LANES, LANES)


def join_rows(x, rows, lons):
    lead = x.shape[:-2]
    x = x.reshape(*lead, lons // LANES, rows, LANES).swapaxes(-3, -2)
    return x.reshape(*lead, rows, lons)


def lane_slice(j):
    return pl.ds(j * LANES, LANES)


def swap_axes8(tiles):
    row = lax.broadcasted_iota(jnp.int32, (8, LANES), 0)
    tiles = list(tiles)
    for step in (4, 2, 1):
        low_half = (row & step) == 0
        for i in range(8):
            if i & step == 0:
                low, high = tiles[i], tiles[i + step]
                tiles[i] = jnp.where(low_half, low, pltpu.roll(high, step, 0))
                tiles[i + step] = jnp.where(low_half, pltpu.roll(low, 8 - step, 0), high)
    return tiles


def level_sums(tiles):
    row = lax.broadcasted_iota(jnp.int32, (8, LANES), 0)
    for step in (1, 2, 4):
        low = (row & step) == 0
        tiles = [
            jnp.where(low, a, b) + pltpu.roll(jnp.where(low, b, a), step, 0) for a, b in zip(tiles[::2], tiles[1::2])
        ]
    return tiles[0]


def unpack_rows(source, target):
    for k in range(8):
        tiles = swap_axes8([source(level * 64 + k * 8) for level in range(8)])
        for half in range(2):
            for r in range(4):
                target[r, :, lane_slice(2 * k + half)] = tiles[4 * half + r]


def east_tiles(tiles):
    lane = lax.broadcasted_iota(jnp.int32, tiles[0].shape, 1)
    turned = [pltpu.roll(x, LANES - 1, 1) for x in tiles]
    count = len(tiles)
    return [jnp.where(lane == LANES - 1, turned[(j + 1) % count], turned[j]) for j in range(count)]


def west_tiles(tiles):
    lane = lax.broadcasted_iota(jnp.int32, tiles[0].shape, 1)
    turned = [pltpu.roll(x, 1, 1) for x in tiles]
    return [jnp.where(lane == 0, turned[j - 1], turned[j]) for j in range(len(tiles))]


def flow_coefficients(u_ref, v_ref, u_rows, v_rows, coef_ref):
    unpack_rows(lambda start: u_ref[pl.ds(start, 8), :], u_rows)
    unpack_rows(lambda start: v_ref[pl.ds(start, 8), :], v_rows)
    for r in range(4):
        u = [u_rows[r, :, lane_slice(j)] for j in range(16)]
        ue = east_tiles(u)
        for j in range(16):
            s = lane_slice(j)
            east = jnp.maximum(ue[j], 0.0)
            west = jnp.minimum(u[j], 0.0)
            south = jnp.minimum(v_rows[r, :, s], 0.0)
            center = 1.0 - east + west + south
            if r < 3:
                north = jnp.maximum(v_rows[r + 1, :, s], 0.0)
                center = center - north
                coef_ref[2, r, :, s] = north
            coef_ref[0, r, :, s] = east
            coef_ref[1, r, :, s] = west
            coef_ref[3, r, :, s] = south
            coef_ref[4, r, :, s] = center


def edge_kernel(a_hbm, last_ref, first_ref, a_ref, sems):
    def incoming(t):
        return pltpu.make_async_copy(a_hbm.at[t], a_ref.at[t], sems.at[t])

    @pl.loop(0, 8)
    def _(t):
        incoming(t).start()

    @pl.loop(0, 8)
    def _(t):
        incoming(t).wait()
        for k in range(8):
            tiles = swap_axes8([a_ref[t, pl.ds(level * 64 + k * 8, 8), :] for level in range(8)])
            for half in range(2):
                first_ref[t, :, lane_slice(2 * k + half)] = tiles[4 * half]
                last_ref[t, :, lane_slice(2 * k + half)] = tiles[4 * half + 3]


def prep_kernel(
    a_hbm, u_hbm, v_hbm, part_hbm, north_hbm, south_hbm, coef_hbm,
    a_ref, u_ref, v_ref, rows_ref, v_rows, part_ref, coef_ref, sems,
):
    faces = [
        pltpu.make_async_copy(u_hbm, u_ref, sems.at[8, 2]),
        pltpu.make_async_copy(v_hbm, v_ref, sems.at[8, 3]),
    ]
    for copy in faces:
        copy.start()

    def incoming(t):
        return pltpu.make_async_copy(a_hbm.at[t], a_ref.at[t], sems.at[t, 3])

    @pl.loop(0, 8)
    def _(t):
        incoming(t).start()

    def copies(t):
        return [
            pltpu.make_async_copy(part_ref.at[t], part_hbm.at[t], sems.at[t, 0]),
            pltpu.make_async_copy(part_ref.at[t, 3], north_hbm.at[t], sems.at[t, 1]),
            pltpu.make_async_copy(part_ref.at[t, 0], south_hbm.at[t], sems.at[t, 2]),
        ]

    for copy in faces:
        copy.wait()
    flow_coefficients(u_ref, v_ref, rows_ref, v_rows, coef_ref)
    coef_copy = pltpu.make_async_copy(coef_ref, coef_hbm, sems.at[8, 0])
    face_copy = pltpu.make_async_copy(v_rows.at[0], south_hbm.at[8], sems.at[8, 1])
    coef_copy.start()
    face_copy.start()

    @pl.loop(0, 8)
    def _(t):
        incoming(t).wait()
        unpack_rows(lambda start: a_ref[t, pl.ds(start, 8), :], rows_ref)
        for r in range(4):
            row = [rows_ref[r, :, lane_slice(j)] for j in range(16)]
            e = east_tiles(row)
            w = west_tiles(row)
            for j in range(16):
                s = lane_slice(j)
                out = row[j] * coef_ref[4, r, :, s] + e[j] * coef_ref[0, r, :, s] - w[j] * coef_ref[1, r, :, s]
                if r < 3:
                    out = out + rows_ref[r + 1, :, s] * coef_ref[2, r, :, s]
                if r > 0:
                    out = out - rows_ref[r - 1, :, s] * coef_ref[3, r, :, s]
                part_ref[t, r, :, s] = out
        for copy in copies(t):
            copy.start()

    @pl.loop(0, 8)
    def _(t):
        for copy in copies(t):
            copy.wait()

    coef_copy.wait()
    face_copy.wait()


def advect_kernel(
    lev_ref, part_hbm, own_last_ref, own_first_ref, own_face_hbm, south_row_ref, south_part_hbm, north_row_ref, north_part_ref,
    coef_hbm, band_hbm, adv_ref, keep_ref, send_ref,
    edge_ref, sum_ref, inside_ref, part_ref, south_part_ref, own_face_ref, coef_ref, band_ref, sems,
):
    tiles = range(16)

    def copies(t):
        return [
            pltpu.make_async_copy(part_hbm.at[t], part_ref.at[t], sems.at[t, 0]),
            pltpu.make_async_copy(south_part_hbm.at[t], south_part_ref.at[t], sems.at[t, 1]),
        ]

    band_copy = pltpu.make_async_copy(band_hbm, band_ref, sems.at[8, 2])
    band_copy.start()
    fixed = [
        pltpu.make_async_copy(coef_hbm, coef_ref, sems.at[8, 0]),
        pltpu.make_async_copy(own_face_hbm.at[8], own_face_ref, sems.at[8, 1]),
    ]
    for copy in fixed:
        copy.start()

    @pl.loop(0, 8)
    def _(t):
        for copy in copies(t):
            copy.start()

    band_copy.wait()
    level = lax.broadcasted_iota(jnp.int32, (8, 2048), 0) + lev_ref[0] * 8
    for r in range(4):
        first = band_ref[0, r : r + 1, :]
        last = band_ref[1, r : r + 1, :]
        inside_ref[r] = jnp.where((level >= first) & (level < last), 1.0, 0.0).astype(F32)

    for copy in fixed:
        copy.wait()
    north_face = jnp.maximum(north_part_ref[8], 0.0)
    edge_ref[0] = jnp.maximum(own_face_ref[...], 0.0)
    edge_ref[1] = jnp.minimum(north_part_ref[8], 0.0)
    edge_ref[2] = north_face
    edge_ref[3] = coef_ref[4, 3] - north_face

    @pl.loop(0, 8)
    def _(t):
        for copy in copies(t):
            copy.wait()
        rows = [[] for _ in range(6)]
        for j in tiles:
            s = lane_slice(j)
            a_south = south_row_ref[t, :, s]
            a_last = own_last_ref[t, :, s]
            a_first = own_first_ref[t, :, s]
            rows[0].append(south_part_ref[t, :, s] + edge_ref[0, :, s] * (a_first - a_south))
            rows[1].append(part_ref[t, 0, :, s] - coef_ref[3, 0, :, s] * a_south)
            rows[2].append(part_ref[t, 1, :, s])
            rows[3].append(part_ref[t, 2, :, s])
            rows[4].append(part_ref[t, 3, :, s] + edge_ref[2, :, s] * (north_row_ref[t, :, s] - a_last))
            rows[5].append(north_part_ref[t, :, s] - edge_ref[1, :, s] * a_last)
        for r in range(4):
            x = rows[r + 1]
            e = east_tiles(x)
            w = west_tiles(x)
            for j in tiles:
                s = lane_slice(j)
                center = coef_ref[4, r, :, s] if r < 3 else edge_ref[3, :, s]
                north = coef_ref[2, r, :, s] if r < 3 else edge_ref[2, :, s]
                out = (
                    x[j] * center
                    + e[j] * coef_ref[0, r, :, s]
                    - w[j] * coef_ref[1, r, :, s]
                    + rows[r + 2][j] * north
                    - rows[r][j] * coef_ref[3, r, :, s]
                )
                adv_ref[r, t, :, s] = out

    @pl.loop(0, 4)
    def _(r):
        for j in tiles:
            s = lane_slice(j)
            inside = inside_ref[r, :, s]
            sum_ref[r, :, s] = level_sums([adv_ref[r, t, :, s] * inside for t in range(8)])

    core = lax.rem(lev_ref[0], 2)
    keep_ref[...] = sum_ref[pl.ds(2 * core, 2)]
    send_ref[...] = sum_ref[pl.ds(2 - 2 * core, 2)]


def halves_of(x):
    high = x.astype(jnp.bfloat16)
    return high, (x - high.astype(F32)).astype(jnp.bfloat16)


def column_kernel(lev_ref, band_ref, flux_ref, inv_ref, gain_ref, matrix_ref):
    lev = lev_ref[0]
    core = lax.rem(lev, 2)
    block = lax.div(lev, 2)
    wide = (64, 128)
    row_pick = (lax.broadcasted_iota(jnp.int32, (64, 8), 0) & 7) == lax.broadcasted_iota(jnp.int32, (64, 8), 1)
    lane = lax.broadcasted_iota(jnp.int32, (16, 128), 1)
    half = jnp.where(lane < 64, core, 1 - core)
    lane_pick = half * 8 + (lane & 7) == lax.broadcasted_iota(jnp.int32, (16, 128), 0)
    same_tracer = (lax.broadcasted_iota(jnp.int32, wide, 0) >> 3) == ((lax.broadcasted_iota(jnp.int32, wide, 1) & 63) >> 3)
    row_pick = jnp.where(row_pick, 1.0, 0.0).astype(F32)
    lane_pick = jnp.where(lane_pick, 1.0, 0.0).astype(F32)
    exact = dict(precision=lax.Precision.HIGHEST, preferred_element_type=F32)
    for r in range(4):
        first = band_ref[0, r : r + 1, :]
        last = band_ref[1, r : r + 1, :]
        scaled = flux_ref[r : r + 1, :] / (last - first).astype(F32)
        inv = inv_ref[r, block, pl.ds(pl.multiple_of(core * 8, 8), 8), :]
        gain = jnp.zeros((8, 2048), F32)
        for k in range(16):
            level_k = block * 16 + k
            weight = jnp.where((first <= level_k) & (level_k < last), scaled, 0.0)
            gain = gain + inv[:, k : k + 1] * weight
        gain_ref[r] = gain
        spread = lax.dot(lax.dot(row_pick, inv, **exact), lane_pick, **exact)
        high, low = halves_of(jnp.where(same_tracer, spread, 0.0))
        matrix_ref[r, 0:64, 0:128] = high
        matrix_ref[r, 0:64, 128:256] = high
        matrix_ref[r, 64:128, 0:128] = low
        matrix_ref[r, 64:128, 128:256] = jnp.zeros_like(low)


def diffuse_kernel(lev_ref, adv_ref, other_ref, band_ref, flux_ref, matrix_ref, out_ref):
    lev = lev_ref[0]
    level = lax.broadcasted_iota(jnp.int32, (8, 2048), 0)
    own_level = level + lev * 8
    other_level = level + (lev + 1 - 2 * lax.rem(lev, 2)) * 8
    for r in range(4):
        first = band_ref[0, r : r + 1, :]
        last = band_ref[1, r : r + 1, :]
        flux = flux_ref[r : r + 1, :]

        def rest(values, levels):
            kept = 1.0 - jnp.where((levels >= first) & (levels < last), flux, 0.0)
            return halves_of((values * kept[None]).reshape(64, 2048))

        own_high, own_low = rest(adv_ref[r], own_level)
        other_high, other_low = rest(other_ref[r], other_level)
        stacked = jnp.concatenate([own_high, other_high, own_low, other_low], axis=0)
        both = lax.dot(matrix_ref[r], stacked, preferred_element_type=F32)
        out_ref[r] = both[:64] + both[64:]


def finish_kernel(lev_ref, base_ref, gain_ref, own_ref, other_ref, forcing_ref, out_ref, sum_ref, done_ref, sems):
    core = lax.rem(lev_ref[0], 2)
    for q in range(2):
        for j in range(16):
            sum_ref[2 * core + q, j] = own_ref[q, :, lane_slice(j)]
            sum_ref[2 - 2 * core + q, j] = other_ref[q, :, lane_slice(j)]

    @pl.loop(0, 8)
    def _(t):
        for k in range(8):
            tiles = []
            for j in (2 * k, 2 * k + 1):
                s = lane_slice(j)
                for r in range(4):
                    total = sum_ref[r, j, pl.ds(t, 8, stride=0), :]
                    forcing = forcing_ref[4 * r + j // 4, :, lane_slice(j % 4)]
                    tiles.append(base_ref[r, t, :, s] + gain_ref[r, :, s] * total + forcing)
            tiles = swap_axes8(tiles)
            for level in range(8):
                done_ref[t, pl.ds(level * 64 + k * 8, 8), :] = tiles[level]
        pltpu.make_async_copy(done_ref.at[t], out_ref.at[t], sems.at[t]).start()

    @pl.loop(0, 8)
    def _(t):
        pltpu.make_async_copy(done_ref.at[t], out_ref.at[t], sems.at[t]).wait()


def pack_kernel(lat_ref, count_ref, values_ref, column_ref, out_ref, line_ref):
    lat = lat_ref[0]
    slot = lax.broadcasted_iota(jnp.int32, (16, LANES), 0)
    line_ref[...] = jnp.zeros((16, LANES), F32)
    line_ref[:, 0:16] = column_ref[...].astype(F32)
    placed = pltpu.roll(line_ref[...], lax.rem(lat, 8) * 16, 1)
    low = jnp.where(lat < 8, placed, 0.0)
    high = jnp.where(lat < 8, 0.0, placed)
    for d in range(16):
        out_ref[d, 0:16, :] = jnp.where(slot < count_ref[d], values_ref[d], 0.0)
        out_ref[d, 16:24, :] = jnp.zeros((8, LANES), F32)
        out_ref[d, 16:17, :] = low[d : d + 1]
        out_ref[d, 17:18, :] = high[d : d + 1]


def forcing_kernel(packed_ref, out_ref):
    lines = packed_ref[0, 16:18, :]
    for source in range(1, 16):
        lines = lines + packed_ref[source, 16:18, :]
    total = jnp.zeros((512, LANES), F32)
    column = lax.broadcasted_iota(jnp.int32, (512, LANES), 0).astype(F32)
    for part in range(2):
        hit = jnp.where(column == lines[part : part + 1], 1.0, 0.0).astype(F32)
        values = jnp.concatenate([packed_ref[8 * part + n, 0:16, :] for n in range(8)], axis=0)
        total = total + lax.dot(hit, values, precision=lax.Precision.HIGHEST, preferred_element_type=F32)
    out_ref[...] = total.T.reshape(16, 8, 512)


def body(adjoint_in, courant_lon, courant_lat, mass_flux, conv_band, diff_inverse, obs_values, obs_column, obs_count):
    tracers, levels, rows, lons = adjoint_in.shape
    lev = lax.axis_index("lev").astype(jnp.int32).reshape(1)
    lat = lax.axis_index("lat").astype(jnp.int32).reshape(1)
    lev_count = lax.axis_size("lev")
    lat_count = lax.axis_size("lat")
    smem = pl.BlockSpec(memory_space=pltpu.SMEM)
    shape = lambda *dims: jax.ShapeDtypeStruct(dims, F32)

    a_view = split_rows(adjoint_in).reshape(tracers, 512, LANES)
    u_view = split_rows(courant_lon).reshape(512, LANES)
    v_view = split_rows(courant_lat).reshape(512, LANES)

    vmem = pl.BlockSpec(memory_space=pltpu.VMEM)
    hbm = pl.BlockSpec(memory_space=pltpu.HBM)
    small = pltpu.CompilerParams(vmem_limit_bytes=16 << 20)
    row_scratch = pltpu.VMEM((4, 8, lons), F32)

    def far(*dims):
        return pltpu.HBM(dims, F32)

    def keep_far(x):
        return pltpu.with_memory_space_constraint(x, pltpu.HBM)

    last_row, first_row = pl.pallas_call(
        edge_kernel,
        in_specs=[hbm],
        out_specs=[vmem] * 2,
        out_shape=[shape(8, 8, lons), shape(8, 8, lons)],
        scratch_shapes=[pltpu.VMEM((8, 512, LANES), F32), pltpu.SemaphoreType.DMA((8,))],
        compiler_params=small,
    )(keep_far(a_view))
    part, to_north, to_south, coef = pl.pallas_call(
        prep_kernel,
        in_specs=[hbm] * 3,
        out_specs=[hbm] * 4,
        out_shape=[far(8, 4, 8, lons), far(8, 8, lons), far(9, 8, lons), far(5, 4, 8, lons)],
        scratch_shapes=[
            pltpu.VMEM((8, 512, LANES), F32), pltpu.VMEM((512, LANES), F32), pltpu.VMEM((512, LANES), F32),
            row_scratch, row_scratch, pltpu.VMEM((8, 4, 8, lons), F32), pltpu.VMEM((5, 4, 8, lons), F32),
            pltpu.SemaphoreType.DMA((9, 4)),
        ],
        compiler_params=small,
    )(keep_far(a_view), keep_far(u_view), keep_far(v_view))
    north = [(i, i + 1) for i in range(lat_count - 1)]
    south = [(i + 1, i) for i in range(lat_count - 1)]
    south_row = lax.ppermute(last_row, "lat", north)
    north_row = lax.ppermute(first_row, "lat", south)
    south_part = lax.ppermute(to_north, "lat", north)
    north_part = lax.ppermute(to_south, "lat", south)

    packed = pl.pallas_call(
        pack_kernel,
        in_specs=[smem, smem, vmem, vmem],
        out_specs=vmem,
        out_shape=shape(16, 24, LANES),
        scratch_shapes=[pltpu.VMEM((16, LANES), F32)],
        compiler_params=small,
    )(lat, obs_count.reshape(16), obs_values.reshape(16, 16, LANES), obs_column.reshape(16, 16))
    packed = lax.all_to_all(packed, "lat", split_axis=0, concat_axis=0, tiled=True)

    forcing = pl.pallas_call(
        forcing_kernel, in_specs=[vmem], out_specs=vmem, out_shape=shape(16, 8, 512), compiler_params=small
    )(packed)
    forcing = lax.all_to_all(forcing, "lev", split_axis=0, concat_axis=0, tiled=True)

    gain, matrix = pl.pallas_call(
        column_kernel,
        in_specs=[smem] + [vmem] * 3,
        out_specs=[vmem] * 2,
        out_shape=[shape(4, 8, lons), jax.ShapeDtypeStruct((4, 128, 256), jnp.bfloat16)],
        compiler_params=small,
    )(lev, conv_band, mass_flux, diff_inverse)

    adv, keep, send = pl.pallas_call(
        advect_kernel,
        in_specs=[smem, hbm, vmem, vmem, hbm, vmem, hbm, vmem, vmem, hbm, hbm],
        out_specs=[vmem] * 3,
        out_shape=[shape(4, 8, 8, lons), shape(2, 8, lons), shape(2, 8, lons)],
        scratch_shapes=[
            row_scratch, row_scratch, row_scratch, pltpu.VMEM((8, 4, 8, lons), F32), pltpu.VMEM((8, 8, lons), F32),
            pltpu.VMEM((8, lons), F32), pltpu.VMEM((5, 4, 8, lons), F32), pltpu.VMEM((2, 4, lons), jnp.int32),
            pltpu.SemaphoreType.DMA((9, 3)),
        ],
        compiler_params=small,
    )(
        lev, keep_far(part), last_row, first_row, keep_far(to_south),
        south_row, south_part, north_row, north_part, keep_far(coef), keep_far(conv_band),
    )

    swap = [(i, i ^ 1) for i in range(lev_count)]
    swapped = lax.ppermute(send, "lev", swap)
    chip_sum = keep + swapped
    blocks = lev_count // 2
    lines = blocks // 2 - 1
    moved = []
    for shift in range(1, lines):
        pairs = []
        for y in range(lines):
            for n in range(4):
                pairs.append((4 * (y + 1) + n, 4 * ((y + shift) % lines + 1) + n))
        moved.append(lax.ppermute(chip_sum, "lev", pairs))
    total = sum(moved, chip_sum)
    adv_other = lax.ppermute(adv, "lev", swap)
    pairs = [(2 * n + c, 2 * (n ^ 1) + c) for n in range(2, blocks) for c in range(2)]
    total = total + lax.ppermute(total, "lev", pairs)
    total_other = lax.ppermute(total, "lev", swap)

    base = pl.pallas_call(
        diffuse_kernel,
        in_specs=[smem] + [vmem] * 5,
        out_specs=vmem,
        out_shape=shape(4, 64, lons),
        compiler_params=small,
    )(lev, adv, adv_other, conv_band, mass_flux, matrix)

    out = pl.pallas_call(
        finish_kernel,
        in_specs=[smem] + [vmem] * 5,
        out_specs=hbm,
        out_shape=shape(tracers, 512, LANES),
        scratch_shapes=[
            pltpu.VMEM((4, 16, 8, LANES), F32), pltpu.VMEM((8, 512, LANES), F32), pltpu.SemaphoreType.DMA((8,))
        ],
        compiler_params=small,
    )(lev, base.reshape(4, 8, 8, lons), gain, total, total_other, forcing)
    return join_rows(out.reshape(tracers, levels, 64, LANES), rows, lons)


def solution(mesh):
    placed = (
        P(None, "lev", "lat", None),
        P("lev", "lat", None),
        P("lev", "lat", None),
        P("lat", None),
        P(None, "lat", None),
        P("lat", None, None, None),
        P("lev", "lat", None, None, None),
        P("lev", "lat", None, None),
        P("lev", "lat", None),
    )

    def step(*args):
        return body(*args)

    step = jax.shard_map(
        step, mesh=mesh, in_specs=placed, out_specs=P(None, "lev", "lat", None), check_vma=False
    )
    return step
```
